512 devices in a mesh: samp: 32 (over x, y_lo, core), var: 16 (over z, y_hi).
Axes of the slice: x: 4, y: 8 (y_hi: 2, y_lo: 4; y = y_hi * 4 + y_lo), z: 8, core: 2. Of those that a mesh axis runs over, the one named last changes fastest.
Arguments:
- genotypes: bfloat16 [16384, 40960], P('samp', 'var'), may hold values from 0 to 2, as said below
- imputed: bfloat16 [16384, 20480], P('samp', 'var'), may hold values from 0 to 2, as said below
- centre: int32 [16384], P('samp'), may hold values from 0 to 21, as said below
- phenotypes: float32 [8, 16384], P(None, 'samp'), may hold values from -6 to 6
- earlier: float32 [8, 16384], P(None, 'samp'), may hold values from -6 to 6
- genetic: float32 [8], replicated, may hold values from 0.2 to 2
- noise: float32 [8], replicated, may hold values from 0.2 to 2
Outputs:
- solution: float32 [8, 16384], P(None, ('samp', 'var'))
- residual: float32 [8, 16384], P(None, ('samp', 'var'))
- scores: float32 [8, 20480], P(None, 'var')
The draws below stay inside these ranges and needn't reach their ends.
Inputs may be any that keep to these rules, and one draw needn't show every extreme that they name: `genotypes`: allele dosages 0, 1 or 2; every variant has its own allele frequency. `imputed`: allele dosages 0, 1 or 2; every variant has its own allele frequency. One of 22 centres; a centre may have no samples.
All inputs are finite; a program needn't handle non-finite values.
Results may differ from the reference program's by a relative error of at most 0.033.
Values may be sent and summed in bfloat16 or wider, within the bound.
No kernel may reach another device: no remote copies, remote signals or barrier semaphores. Data moves between devices by JAX's collectives and lax.ppermute only.
A program may use at most 64 MiB of HBM per device.

```python
import math
import jax
import jax.numpy as jnp
from jax import lax

M = 40960
IMP = 20480
PHENO = 8
CENTRES = 22
ITERS = 2
SAMPLES = 16384


def dosages(key, rows, columns):
    freq = jax.random.randint(jax.random.fold_in(key, 1), (1, columns), 2, 51)
    first = jax.random.randint(jax.random.fold_in(key, 2), (rows, columns), 0, 100)
    second = jax.random.randint(jax.random.fold_in(key, 3), (rows, columns), 0, 100)
    return ((first < freq).astype(jnp.int32) + (second < freq).astype(jnp.int32)).astype(jnp.float32)


def draw_genotypes(key, part):
    return dosages(jax.random.fold_in(key, 11), SAMPLES, M).astype(jnp.bfloat16)


def draw_imputed(key, part):
    return dosages(jax.random.fold_in(key, 23), SAMPLES, IMP).astype(jnp.bfloat16)


def draw_centre(key, part):
    base = jax.random.fold_in(key, 37)
    shuffled = jax.random.permutation(jax.random.fold_in(base, 1), CENTRES - 2).astype(jnp.int32) + 1
    opened = jnp.concatenate([jnp.zeros((1,), jnp.int32), shuffled[4:], jnp.full((1,), CENTRES - 1, jnp.int32)])
    picks = jax.random.randint(jax.random.fold_in(base, 2), (SAMPLES,), 0, CENTRES - 4)
    centre_ids = opened[picks]
    chosen = jax.random.permutation(jax.random.fold_in(base, 3), SAMPLES)
    centre_ids = centre_ids.at[chosen[0]].set(0)
    centre_ids = centre_ids.at[chosen[1]].set(CENTRES - 1)
    return centre_ids.astype(jnp.int32)


def level_of(own_key, dims, split, smallest, top_value):
    loudness = 1.0
    for axis_at, parts in split:
        draws = jax.random.uniform(jax.random.fold_in(jax.random.fold_in(own_key, 6), axis_at), (parts,), jnp.float32, smallest / len(split), top_value / len(split))
        loudness = loudness * jnp.repeat(jnp.exp(draws), dims[axis_at] // parts).reshape((-1,) + (1,) * (len(dims) - 1 - axis_at))
    return loudness


def scatter_about(rng, extent, scale, limit, cuts=(), kind=jnp.bfloat16):
    array = scale * jax.random.normal(rng, extent, jnp.float32)
    if cuts:
        array = array * level_of(rng, extent, cuts, -0.22, 0.18)
    return jnp.clip(array, -limit, limit).astype(kind)


def setup_inputs(seed: int = 0) -> dict:
    key_list = jax.random.split(jax.random.key(seed), 8)
    genotypes = draw_genotypes(jax.random.fold_in(key_list[7], 71), 0)
    imputed = draw_imputed(jax.random.fold_in(key_list[7], 71), 0)
    centre = draw_centre(jax.random.fold_in(key_list[7], 71), 0)
    phenotypes = scatter_about(key_list[3], (PHENO, SAMPLES), 1.0, 6.0, ((1, 32),), jnp.float32)
    earlier = scatter_about(key_list[4], (PHENO, SAMPLES), 1.0, 6.0, ((1, 32),), jnp.float32)
    genetic = jnp.clip(jnp.exp(jax.random.uniform(key_list[5], (PHENO,), jnp.float32, math.log(0.2), math.log(2.0))), 0.2, 2.0)
    noise = jnp.clip(jnp.exp(jax.random.uniform(key_list[6], (PHENO,), jnp.float32, math.log(0.2), math.log(2.0))), 0.2, 2.0)
    return {"genotypes": genotypes, "imputed": imputed, "centre": centre, "phenotypes": phenotypes, "earlier": earlier, "genetic": genetic, "noise": noise}


def column_stats(genotypes):
    block_width = math.gcd(M, 4096)
    means = []
    scales = []
    for column_start in range(0, M, block_width):
        values = genotypes[:, column_start:column_start + block_width].astype(jnp.float32)
        mean_col = lax.optimization_barrier(jnp.sum(values, axis=0)) / SAMPLES
        var_col = lax.optimization_barrier(jnp.sum(values * values, axis=0)) / SAMPLES - mean_col * mean_col
        means.append(mean_col)
        scales.append(lax.rsqrt(var_col + 1e-05))
    return (means, scales)

def operate(direction, genotypes, means, scales, genetic, noise):
    block_width = math.gcd(M, 4096)
    low = direction.astype(jnp.bfloat16)
    back = jnp.zeros(direction.shape, jnp.float32)
    for index, column_start in enumerate(range(0, M, block_width)):
        values = genotypes[:, column_start:column_start + block_width].astype(jnp.float32)
        standard = ((values - means[index][None, :]) * scales[index][None, :]).astype(jnp.bfloat16)
        projected = jnp.dot(low, standard, preferred_element_type=jnp.float32)
        scaled = (projected * (genetic / M)[:, None]).astype(jnp.bfloat16)
        back = back + lax.dot_general(scaled, standard, (((1,), (1,)), ((), ())), preferred_element_type=jnp.float32)
    return back + noise[:, None] * direction

def reference(genotypes, imputed, centre, phenotypes, earlier, genetic, noise):
    means, scales = column_stats(genotypes)
    onehot = (centre[:, None] == jnp.arange(CENTRES, dtype=jnp.int32)[None, :]).astype(jnp.float32)
    centre_sum = jnp.dot(phenotypes, onehot, precision=lax.Precision.HIGHEST)
    counts = lax.optimization_barrier(jnp.sum(onehot, axis=0))
    centre_mean = centre_sum / jnp.maximum(counts, 1.0)[None, :]
    centred = phenotypes - jnp.dot(centre_mean, onehot.T, precision=lax.Precision.HIGHEST)
    solution = jnp.zeros_like(centred)
    residual = centred
    direction = centred
    norm_now = lax.optimization_barrier(jnp.sum(residual * residual, axis=1))
    for step in range(ITERS):
        image = operate(direction, genotypes, means, scales, genetic, noise)
        alpha = norm_now / lax.optimization_barrier(jnp.sum(direction * image, axis=1))
        solution = solution + alpha[:, None] * direction
        residual = residual - alpha[:, None] * image
        if step + 1 < ITERS:
            norm_next = lax.optimization_barrier(jnp.sum(residual * residual, axis=1))
            direction = residual + (norm_next / norm_now)[:, None] * direction
            norm_now = norm_next
    earlier_var = lax.optimization_barrier(jnp.sum(earlier * earlier, axis=1)) / SAMPLES + 1e-05
    earlier_sum = lax.optimization_barrier(jnp.sum(earlier, axis=1))
    imp_width = math.gcd(IMP, 4096)
    pieces = []
    for column_start in range(0, IMP, imp_width):
        dosage = imputed[:, column_start:column_start + imp_width].astype(jnp.float32)
        imp_mean = lax.optimization_barrier(jnp.sum(dosage, axis=0)) / SAMPLES
        imp_var = lax.optimization_barrier(jnp.sum(dosage * dosage, axis=0)) / SAMPLES - imp_mean * imp_mean + 1e-05
        cross = jnp.dot(earlier, dosage, precision=lax.Precision.HIGHEST) - earlier_sum[:, None] * imp_mean[None, :]
        pieces.append(cross / jnp.sqrt(SAMPLES * imp_var[None, :] * earlier_var[:, None]))
    scores = jnp.concatenate(pieces, axis=1)
    return (solution, residual, scores)
```

```python
import jax
import jax.numpy as jnp
from jax import lax
from jax.sharding import PartitionSpec as P

M = 40960
CENTRES = 22
SLOTS = 12
LANE = 128
BASE = 4096.0


def split(x, parts):
    out = []
    for _ in range(parts):
        top = lax.reduce_precision(x, 8, 7)
        out.append(top.astype(jnp.bfloat16))
        x = x - top
    return out


def exact_dot(x, y, parts=3):
    pieces = jnp.concatenate(split(x, parts), axis=0)
    full = jnp.dot(pieces, y, preferred_element_type=jnp.float32)
    return jnp.sum(full.reshape(parts, x.shape[0], -1), axis=0)


def exchange(x, axis):
    return lax.all_to_all(x, axis, 0, 0, tiled=True)


def share(x, axis):
    return exchange(jnp.broadcast_to(x[None], (lax.axis_size(axis),) + x.shape), axis)


def in_lanes(columns):
    rows = columns[0].shape[0]
    lane = lax.broadcasted_iota(jnp.int32, (rows, LANE), 1)
    out = jnp.zeros((rows, LANE), jnp.float32)
    for at, column in enumerate(columns):
        out = jnp.where(lane == at, column, out)
    return out


def blocks(x):
    rows, columns = x.shape
    return x.reshape(rows, columns // LANE, LANE).transpose(1, 0, 2)


def flat(x):
    count, rows, _ = x.shape
    return x.transpose(1, 0, 2).reshape(rows, count * LANE)


def shards(genotypes, imputed, centre, phenotypes, earlier, genetic, noise):
    rows, model = genotypes.shape
    other = imputed.shape[1]
    pheno = phenotypes.shape[0]
    groups = lax.axis_size("samp")
    total = rows * groups
    model_blocks, other_blocks = model // LANE, other // LANE
    spare = groups - model_blocks - other_blocks
    me, mine = lax.axis_index("samp"), lax.axis_index("var")
    genetic = genetic[:, None] / M
    noise = noise[:, None]
    bf16, f32 = jnp.bfloat16, jnp.float32

    hot = centre[None, :] == lax.broadcasted_iota(jnp.int32, (2 * SLOTS, rows), 0)
    pairs = jnp.where(hot[:SLOTS], 1.0, jnp.where(hot[SLOTS:], BASE, 0.0)).astype(bf16)
    pieces = jnp.concatenate(split(phenotypes, 3) + [pairs], axis=0)
    product = jnp.dot(pieces, genotypes, preferred_element_type=f32)
    by_model = product[:pheno] + product[pheno : 2 * pheno] + product[2 * pheno : 3 * pheno]
    packed = product[3 * pheno :]
    square_row = jnp.where(lax.broadcasted_iota(jnp.int32, (SLOTS, rows), 0) == CENTRES - SLOTS, BASE, 0.0)
    packed = packed + jnp.dot(square_row.astype(bf16), genotypes * genotypes, preferred_element_type=f32)
    lane = lax.broadcasted_iota(jnp.int32, (rows, LANE), 1)
    spots = [(lane == centre[:, None] + at).astype(bf16) for at in (0, 32, 64)]
    half = pheno // 2
    table = (
        exact_dot(phenotypes[:half], spots[0])
        + exact_dot(phenotypes[half:], spots[1])
        + jnp.dot(jnp.ones((half, rows), bf16), spots[2], preferred_element_type=f32)
    )
    by_other = exact_dot(earlier, imputed)
    dosage = imputed.astype(f32)
    other_sum = jnp.sum(dosage, axis=0, keepdims=True)
    other_sq = jnp.sum(dosage * dosage, axis=0, keepdims=True)
    moments = in_lanes([jnp.sum(earlier, 1, keepdims=True), jnp.sum(earlier * earlier, 1, keepdims=True)])
    first = jnp.concatenate([blocks(by_model), blocks(packed)], axis=1)
    second = jnp.concatenate(
        [
            blocks(by_other),
            jnp.broadcast_to(moments[None], (other_blocks, pheno, LANE)),
            blocks(jnp.concatenate([other_sum, other_sq, other_sum, other_sq], axis=0)),
        ],
        axis=1,
    )
    chunk = jnp.concatenate([first, second, jnp.zeros((spare,) + first.shape[1:], f32)], axis=0)
    chunk = jnp.concatenate([chunk, jnp.broadcast_to(table[None], (groups, half, LANE))], axis=1)
    got = exchange(chunk, "samp")

    raw = jnp.sum(got, axis=0)
    high = jnp.floor(got[:, pheno : pheno + SLOTS] * (1.0 / BASE))
    low = got[:, pheno : pheno + SLOTS] - BASE * high
    counts = jnp.concatenate([jnp.sum(low, axis=0), jnp.sum(high, axis=0)], axis=0)
    table = raw[-half:]
    centre_sum = jnp.concatenate([table[:, :CENTRES], table[:, 32 : 32 + CENTRES]], axis=0)
    centre_count = table[:1, 64 : 64 + CENTRES]
    centre_mean = centre_sum / jnp.maximum(centre_count, 1.0)
    left = jnp.sum(centre_sum - centre_mean * centre_count, axis=1, keepdims=True)
    per_centre = counts[:CENTRES]
    mean = jnp.sum(per_centre, axis=0, keepdims=True) / total
    scale = lax.rsqrt(counts[CENTRES : CENTRES + 1] / total - mean * mean + 1e-05)
    proj0 = raw[:pheno] - jnp.dot(centre_mean, per_centre, precision=lax.Precision.HIGHEST)
    proj0 = (proj0 - left * mean) * scale
    back0 = lax.reduce_precision(proj0 * scale * genetic, 8, 7)
    shift0 = jnp.sum(back0 * mean, axis=1, keepdims=True)

    cross, moments = raw[:pheno], raw[pheno : 2 * pheno]
    other_mean = raw[2 * pheno : 2 * pheno + 1] / total
    other_var = raw[2 * pheno + 1 : 2 * pheno + 2] / total - other_mean * other_mean + 1e-05
    earlier_var = moments[:, 1:2] / total + 1e-05
    score = (cross - moments[:, :1] * other_mean) / jnp.sqrt(total * other_var * earlier_var)

    owner = me < model_blocks
    top = jnp.where(owner, back0, lax.reduce_precision(score, 8, 7))
    shift_parts = [x.astype(f32) for x in split(shift0, 3)]
    rest = jnp.where(owner, in_lanes(shift_parts), score - lax.reduce_precision(score, 8, 7))
    got = share(jnp.concatenate([top, rest], axis=0).astype(bf16), "samp")
    scores = flat(
        got[model_blocks : model_blocks + other_blocks, :pheno].astype(f32)
        + got[model_blocks : model_blocks + other_blocks, pheno:].astype(f32)
    )

    def back(got):
        values = flat(got[:model_blocks, :pheno])
        extra = jnp.sum(got[:model_blocks, pheno:].astype(f32), axis=0)
        part = lax.dot_general(values, genotypes, (((1,), (1,)), ((), ())), preferred_element_type=f32)
        return part - jnp.sum(extra[:, :3], axis=1, keepdims=True), extra

    part, _ = back(got)
    hot = (centre[None, :] == lax.broadcasted_iota(jnp.int32, (CENTRES, rows), 0)).astype(f32)
    start = phenotypes - jnp.dot(centre_mean, hot, precision=lax.Precision.HIGHEST)
    image = jnp.sum(share(part, "var"), axis=0)

    image_low = lax.reduce_precision(image, 8, 7)
    by_model = blocks(jnp.dot(image_low.astype(bf16), genotypes, preferred_element_type=f32))
    by_model = jnp.concatenate([by_model, jnp.zeros((groups - model_blocks, pheno, LANE), f32)], axis=0)
    grams = in_lanes(
        [jnp.sum(x, axis=1, keepdims=True) for x in (start * start, start * image, image * image, image_low)]
    )
    grams = jnp.broadcast_to(grams[None], (groups, pheno, LANE))
    raw = jnp.sum(exchange(jnp.concatenate([by_model, grams], axis=1), "samp"), axis=0)
    gram = [raw[pheno:, at : at + 1] for at in range(4)]
    norm0 = gram[0]
    rate = gram[1] / norm0
    alpha0 = 1.0 / (rate + noise)
    norm1 = alpha0 * alpha0 * (gram[2] - rate * gram[1])
    on_image, on_start = -alpha0, alpha0 * rate + norm1 / norm0
    length = on_image * on_image * gram[2] + 2.0 * on_image * on_start * gram[1] + on_start * on_start * norm0
    proj1 = (raw[:pheno] - gram[3] * mean) * scale
    proj = on_image * proj1 + on_start * proj0
    back1 = lax.reduce_precision(proj * scale * genetic, 8, 7)
    shift1 = jnp.sum(back1 * mean, axis=1, keepdims=True)
    energy = jnp.sum(proj * proj, axis=1, keepdims=True) * genetic
    rest = in_lanes([x.astype(f32) for x in split(shift1, 3) + split(energy, 3)])
    got = share(jnp.concatenate([back1, rest], axis=0).astype(bf16), "samp")

    part, extra = back(got)
    energy = jnp.sum(extra[:, 3:6], axis=1, keepdims=True)
    ways = lax.axis_size("var")
    width = rows // ways
    per = LANE // width
    tiles = blocks(part)
    lane = lax.broadcasted_iota(jnp.int32, (ways, pheno, LANE), 2)
    peer = lax.broadcasted_iota(jnp.int32, (ways, pheno, LANE), 0)
    tiles = jnp.broadcast_to(tiles[:, None], (ways // per, per, pheno, LANE)).reshape(ways, pheno, LANE)
    spot = lax.rem(width * lax.rem(peer, per) + width, LANE)
    got = jnp.sum(exchange(jnp.where(lane == spot, energy[None], tiles), "var"), axis=0)
    lane = lax.broadcasted_iota(jnp.int32, (pheno, LANE), 1)
    offset = width * lax.rem(mine, per)
    curve = jnp.sum(jnp.where(lane == lax.rem(offset + width, LANE), got, 0.0), axis=1, keepdims=True)
    last = lax.dynamic_slice_in_dim(got, offset, width, 1)
    start = lax.dynamic_slice_in_dim(start, mine * width, width, 1)
    image = lax.dynamic_slice_in_dim(image, mine * width, width, 1)
    alpha1 = norm1 / (curve + noise * length)
    direction = on_image * image + on_start * start
    residual = -alpha0 * (image - rate * start) - alpha1 * (last + noise * direction)
    return (alpha0 * start + alpha1 * direction, residual, scores)


def solution(mesh):
    in_specs = (
        P("samp", "var"),
        P("samp", "var"),
        P("samp"),
        P(None, "samp"),
        P(None, "samp"),
        P(),
        P(),
    )
    out_specs = (P(None, ("samp", "var")), P(None, ("samp", "var")), P(None, "var"))
    return jax.shard_map(shards, mesh=mesh, in_specs=in_specs, out_specs=out_specs, check_vma=False)
```

```python
import functools

import jax
import jax.numpy as jnp
from jax import lax
from jax.experimental import pallas as pl
from jax.experimental.pallas import tpu as pltpu
from jax.sharding import PartitionSpec as P

M = 40960
CENTRES = 22
SLOTS = 12
LANE = 128
BASE = 4096.0
STEPS = 5
GRANT = 16 << 20
BF16, F32 = jnp.bfloat16, jnp.float32
NT = (((1,), (1,)), ((), ()))


def split(x, parts):
    out = []
    for _ in range(parts):
        top = x.astype(BF16)
        out.append(top)
        x = x - top.astype(F32)
    return out


def dot(x, y):
    return jnp.dot(x, y, preferred_element_type=F32)


def dot_t(x, y):
    return lax.dot_general(x, y, NT, preferred_element_type=F32)


def iota(shape, dim):
    return lax.broadcasted_iota(jnp.int32, shape, dim)


def row_sum(x):
    return jnp.sum(x, axis=1, keepdims=True)


def in_lanes(columns):
    lane = iota((columns[0].shape[0], LANE), 1)
    out = jnp.zeros((columns[0].shape[0], LANE), F32)
    for at, column in enumerate(columns):
        out = jnp.where(lane == at, column, out)
    return out


def cut(x, at):
    return x[:, at * LANE : (at + 1) * LANE]


def gather_kernel(
    gen_hbm, imp_hbm, centre_hbm, phen_hbm, earl_hbm, genetic_hbm, noise_hbm,
    out_ref, gen_ref, cols_ref, imp_ref, centre_ref, phen_ref, earl_ref, scal_ref, sem,
):
    rows, model = gen_ref.shape
    groups, pheno = out_ref.shape[0], phen_ref.shape[0]
    wide, narrow = model // STEPS, imp_ref.shape[1] // STEPS
    own, other = wide // LANE, narrow // LANE
    first_other = own * STEPS
    small = [(centre_hbm, centre_ref), (phen_hbm, phen_ref), (earl_hbm, earl_ref)]
    small += [(genetic_hbm, scal_ref.at[0]), (noise_hbm, scal_ref.at[1])]
    copies = [pltpu.make_async_copy(x, y, sem.at[i]) for i, (x, y) in enumerate(small)]
    for step in range(STEPS):
        cols = pl.ds(step * wide, wide)
        copies.append(pltpu.make_async_copy(gen_hbm.at[:, cols], gen_ref.at[:, cols], sem.at[5 + 2 * step]))
        cols = pl.ds(step * narrow, narrow)
        copies.append(pltpu.make_async_copy(imp_hbm.at[:, cols], imp_ref.at[:, cols], sem.at[6 + 2 * step]))
    for copy in copies:
        copy.start()

    spot = iota((LANE, rows), 0)
    slot = iota((16, rows), 0)
    for copy in copies[:3]:
        copy.wait()
    centre = centre_ref[...]
    pairs = jnp.where(slot < SLOTS, jnp.where(centre == slot, 1.0, jnp.where(centre == slot + SLOTS, BASE, 0.0)), 0.0)
    pieces = [p.astype(F32) for p in split(phen_ref[...], 3)]
    phen = jnp.concatenate(pieces + [jnp.ones((pheno, rows), F32)], axis=0).astype(BF16)
    left = jnp.concatenate(pieces + [pairs], axis=0).astype(BF16)
    left_square = jnp.where(slot == CENTRES - SLOTS, BASE, 0.0).astype(BF16)
    earl = earl_ref[...]
    pieces = [p.astype(F32) for p in split(earl, 3)]
    right = jnp.concatenate(pieces + [jnp.ones((pheno, rows), F32)], axis=0).astype(BF16)
    right_square = jnp.ones((16, rows), BF16)
    sums = []
    for at in (0, 32, 64):
        full = dot_t(phen, jnp.where(spot == centre + at, 1.0, 0.0).astype(BF16))
        sums.append(full[24:32] if at == 64 else full[0:8] + full[8:16] + full[16:24])
    row = iota((pheno, LANE), 0)
    table = jnp.where(row < 4, 0.0, pltpu.roll(sums[0], 4, 0) + sums[1] + sums[2])
    moments = in_lanes([row_sum(earl), row_sum(earl * earl)])
    for at in range(first_other + other * STEPS, groups):
        out_ref[at, 0:8, :] = jnp.zeros((8, LANE), F32)
        out_ref[at, 8:16, :] = jnp.zeros((8, LANE), F32)
        out_ref[at, 16:24, :] = table
    for copy in copies[3:5]:
        copy.wait()
    for at in range(2):
        column = jnp.zeros((pheno, LANE), F32)
        for k in range(pheno):
            column = jnp.where(row == k, scal_ref[at, k], column)
        cols_ref[at] = column * (1.0 / M) if at == 0 else column

    for step in range(STEPS):
        copies[5 + 2 * step].wait()
        gen = gen_ref[:, step * wide : (step + 1) * wide]
        full = dot(left, gen)
        by_model = full[0:8] + full[8:16] + full[16:24]
        packed = full[24:40] + dot(left_square, gen * gen)
        for at in range(own):
            block = step * own + at
            out_ref[block, 0:8, :] = cut(by_model, at)
            out_ref[block, 8:16, :] = cut(packed[0:8], at)
            out_ref[block, 16:24, :] = cut(packed[8:16], at) + table
        copies[6 + 2 * step].wait()
        imp = imp_ref[:, step * narrow : (step + 1) * narrow]
        full = dot(right, imp)
        by_other = full[0:8] + full[8:16] + full[16:24]
        square = dot(right_square, imp * imp)[0:8]
        for at in range(other):
            block = first_other + step * other + at
            counts = jnp.where(row == 0, cut(full[24:32], at), jnp.where(row == 1, cut(square, at), table))
            out_ref[block, 0:8, :] = cut(by_other, at)
            out_ref[block, 8:16, :] = moments
            out_ref[block, 16:24, :] = counts


def gather(groups, *operands):
    genotypes, imputed, _, phenotypes = operands[:4]
    rows, model = genotypes.shape
    other = imputed.shape[1]
    pheno = phenotypes.shape[0]
    return pl.pallas_call(
        gather_kernel,
        out_shape=[
            pltpu.VMEM((groups, 24, LANE), F32),
            pltpu.VMEM((rows, model), BF16),
            pltpu.VMEM((2, pheno, LANE), F32),
        ],
        in_specs=[pl.BlockSpec(memory_space=pltpu.HBM)] * len(operands),
        out_specs=[pl.BlockSpec(memory_space=pltpu.VMEM)] * 3,
        scratch_shapes=[
            pltpu.VMEM((rows, other), BF16),
            pltpu.VMEM((1, rows), jnp.int32),
            pltpu.VMEM((pheno, rows), F32),
            pltpu.VMEM((pheno, rows), F32),
            pltpu.SMEM((2, pheno), F32),
            pltpu.SemaphoreType.DMA((5 + 2 * STEPS,)),
        ],
        compiler_params=pltpu.CompilerParams(vmem_limit_bytes=GRANT),
    )(*[pltpu.with_memory_space_constraint(x, pltpu.HBM) for x in operands])


def call(kernel, outs, *operands):
    return pl.pallas_call(
        kernel,
        out_shape=[
            jax.ShapeDtypeStruct(shape, kind) if last else pltpu.VMEM(shape, kind) for shape, kind, last in outs
        ],
        in_specs=[pl.BlockSpec(memory_space=pltpu.VMEM)] * len(operands),
        out_specs=[pl.BlockSpec(memory_space=pltpu.VMEM)] * len(outs),
        compiler_params=pltpu.CompilerParams(vmem_limit_bytes=GRANT),
    )(*[pltpu.with_memory_space_constraint(x, pltpu.VMEM) for x in operands])


def owner_kernel(total, model_blocks, got_ref, cols_ref, send_ref, keep_ref):
    groups, pheno = got_ref.shape[0], 8
    got = got_ref[...]
    raw = jnp.sum(got, axis=0)
    pack = got[:, 8:24, :]
    high = jnp.floor(pack * (1.0 / BASE))
    low = jnp.sum(pack - BASE * high, axis=0)
    high = jnp.sum(high, axis=0)
    table = raw[16:24]
    row = iota((pheno, LANE), 0)
    lane = iota((pheno, LANE), 1)
    sums = jnp.where(row < 4, pltpu.roll(table, 4, 0), pltpu.roll(table, LANE - 32, 1))
    sums = jnp.where(lane < CENTRES, sums, 0.0)
    count = pltpu.roll(table, LANE - 64, 1)
    count = jnp.where(row < 4, pltpu.roll(count, 4, 0), count)
    count = jnp.where(lane < CENTRES, count, 0.0)
    centre_mean = sums / jnp.maximum(count, 1.0)
    left = row_sum(sums - centre_mean * count)
    proj = raw[0:8]
    seen = jnp.zeros((1, LANE), F32)
    for c in range(CENTRES):
        line = low[c : c + 1] if c < SLOTS else high[c - SLOTS : c - SLOTS + 1]
        seen = seen + line
        proj = proj - centre_mean[:, c : c + 1] * line
    mean = seen / total
    scale = lax.rsqrt(high[CENTRES - SLOTS : CENTRES - SLOTS + 1] / total - mean * mean + 1e-05)
    proj = (proj - left * mean) * scale
    back = proj * scale * cols_ref[0]
    m0, m1, m2 = [x.astype(F32) for x in split(mean, 3)]
    lines = jnp.where(row == 0, m0, jnp.where(row == 1, m1, jnp.where(row == 2, m2, 0.0)))

    other_mean = raw[16:17] / total
    other_var = raw[17:18] / total - other_mean * other_mean + 1e-05
    moments = raw[8:16]
    earlier_var = moments[:, 1:2] / total + 1e-05
    score = (raw[0:8] - moments[:, 0:1] * other_mean) / jnp.sqrt(total * other_var * earlier_var)
    score_top = score.astype(BF16).astype(F32)

    owner = lax.axis_index("samp") < model_blocks
    send = jnp.concatenate([jnp.where(owner, back, score_top), jnp.where(owner, lines, score - score_top)], axis=0)
    send_ref[...] = jnp.broadcast_to(send.astype(BF16)[None], (groups, 16, LANE))
    keep_ref[0] = proj
    keep_ref[1] = jnp.broadcast_to(mean, (pheno, LANE))
    keep_ref[2] = jnp.broadcast_to(scale, (pheno, LANE))
    keep_ref[3] = centre_mean


def back_product(got_ref, gen_ref, model_blocks):
    acc = None
    for at in range(0, model_blocks, 2):
        values = jnp.concatenate([got_ref[at], got_ref[at + 1]], axis=1)
        part = dot_t(values, gen_ref[:, at * LANE : (at + 2) * LANE])
        acc = part if acc is None else acc + part
    return acc[0:8]


def back0_kernel(model_blocks, other_blocks, got_ref, gen_ref, centre_ref, phen_ref, keep_ref, send_ref, start_ref, mean_ref, score_ref):
    ways = send_ref.shape[0]
    pheno, rows = phen_ref.shape
    shift = jnp.zeros((pheno, LANE), F32)
    for at in range(model_blocks):
        block = got_ref[at].astype(F32)
        mean = block[8:9] + block[9:10] + block[10:11]
        mean_ref[:, at * LANE : (at + 1) * LANE] = mean
        shift = shift + block[0:8] * mean
    part = back_product(got_ref, gen_ref, model_blocks) - row_sum(shift)
    half = rows // 2
    send = jnp.concatenate([part[:, :half], part[:, half:]], axis=0).astype(BF16)
    send_ref[...] = jnp.broadcast_to(send[None], (ways, 16, half))
    for at in range(other_blocks):
        block = got_ref[model_blocks + at].astype(F32)
        score_ref[:, at * LANE : (at + 1) * LANE] = block[0:8] + block[8:16]
    centre = centre_ref[...]
    start = phen_ref[...]
    centre_mean = keep_ref[3]
    for c in range(CENTRES):
        start = start - jnp.where(centre == c, centre_mean[:, c : c + 1], 0.0)
    start_ref[...] = start


def project_kernel(model_blocks, got_ref, gen_ref, start_ref, mean_ref, send_ref, image_ref):
    groups = send_ref.shape[0]
    pheno, rows = start_ref.shape
    half = rows // 2
    both = jnp.sum(got_ref[...].astype(F32), axis=0)
    image = jnp.concatenate([both[0:8], both[8:16]], axis=1)
    image_ref[...] = image
    start = start_ref[...]
    parts = []
    for x in (start * start, start * image, image * image):
        parts += [p.astype(F32) for p in split(row_sum(x), 3)]
    grams = in_lanes(parts)
    total = row_sum(image)
    left = jnp.concatenate([p.astype(F32) for p in split(image, 2)], axis=0).astype(BF16)
    for at in range(0, model_blocks, 4):
        cols = slice(at * LANE, (at + 4) * LANE)
        full = dot(left, gen_ref[:, cols])
        full = full[0:8] + full[8:16] - total * mean_ref[:, cols]
        for b in range(4):
            send_ref[at + b] = jnp.concatenate([cut(full, b), grams], axis=0).astype(BF16)
    rest = jnp.concatenate([jnp.zeros((pheno, LANE), F32), grams], axis=0).astype(BF16)
    for at in range(model_blocks, groups):
        send_ref[at] = rest


def next_kernel(got_ref, keep_ref, cols_ref, send_ref, coef_ref):
    groups = got_ref.shape[0]
    raw = jnp.sum(got_ref[...].astype(F32), axis=0)
    extra = raw[8:16]
    norm0, cross, square = [row_sum(extra[:, 3 * at : 3 * at + 3]) for at in range(3)]
    genetic, noise = cols_ref[0], cols_ref[1]
    rate = cross / norm0
    alpha0 = 1.0 / (rate + noise)
    norm1 = alpha0 * alpha0 * (square - rate * cross)
    on_image, on_start = -alpha0, alpha0 * rate + norm1 / norm0
    length = on_image * on_image * square + 2.0 * on_image * on_start * cross + on_start * on_start * norm0
    proj = on_image * (raw[0:8] * keep_ref[2]) + on_start * keep_ref[0]
    back = proj * keep_ref[2] * genetic
    energy = row_sum(proj * proj) * genetic
    lines = in_lanes([p.astype(F32)[:, 0:1] for p in split(energy, 3)])
    send = jnp.concatenate([back, lines], axis=0).astype(BF16)
    send_ref[...] = jnp.broadcast_to(send[None], (groups, 16, LANE))
    coef_ref[...] = in_lanes([x[:, 0:1] for x in (rate, alpha0, norm1, on_image, on_start, length)])


def back1_kernel(model_blocks, got_ref, gen_ref, mean_ref, send_ref):
    ways, pheno, _ = send_ref.shape
    rows = gen_ref.shape[0]
    width = rows // ways
    per = LANE // width
    shift = jnp.zeros((pheno, LANE), F32)
    extra = jnp.zeros((pheno, LANE), F32)
    for at in range(model_blocks):
        block = got_ref[at].astype(F32)
        shift = shift + block[0:8] * mean_ref[:, at * LANE : (at + 1) * LANE]
        extra = extra + block[8:16]
    energy = row_sum(extra)
    part = back_product(got_ref, gen_ref, model_blocks) - row_sum(shift)
    lane = iota((pheno, LANE), 1)
    for peer in range(ways):
        spot = (width * (peer % per) + width) % LANE
        send_ref[peer] = jnp.where(lane == spot, energy, cut(part, peer // per))


def finish_kernel(got_ref, start_ref, image_ref, coef_ref, cols_ref, out_ref, residual_ref):
    ways, pheno, _ = got_ref.shape
    rows = start_ref.shape[1]
    width = rows // ways
    per = LANE // width
    mine = lax.axis_index("var")
    tile, at = lax.div(mine, per), lax.rem(mine, per)
    got = jnp.sum(got_ref[...], axis=0)
    lane = iota((pheno, LANE), 1)
    curve = row_sum(jnp.where(lane == lax.rem(at * width + width, LANE), got, 0.0))
    start = jnp.zeros((pheno, LANE), F32)
    image = jnp.zeros((pheno, LANE), F32)
    for t in range(rows // LANE):
        start = jnp.where(tile == t, cut(start_ref[...], t), start)
        image = jnp.where(tile == t, cut(image_ref[...], t), image)
    coef, noise = coef_ref[...], cols_ref[1]
    rate, alpha0, norm1, on_image, on_start, length = [coef[:, i : i + 1] for i in range(6)]
    alpha1 = norm1 / (curve + noise * length)
    direction = on_image * image + on_start * start
    residual = -alpha0 * (image - rate * start) - alpha1 * (got + noise * direction)
    answer = alpha0 * start + alpha1 * direction
    out, left = answer[:, :width], residual[:, :width]
    for a in range(1, per):
        out = jnp.where(at == a, answer[:, a * width : (a + 1) * width], out)
        left = jnp.where(at == a, residual[:, a * width : (a + 1) * width], left)
    out_ref[...] = out
    residual_ref[...] = left


def exchange(x, axis):
    return lax.all_to_all(x, axis, 0, 0, tiled=True)


def shards(genotypes, imputed, centre, phenotypes, earlier, genetic, noise):
    rows, model = genotypes.shape
    other = imputed.shape[1]
    pheno = phenotypes.shape[0]
    groups, ways = lax.axis_size("samp"), lax.axis_size("var")
    model_blocks, other_blocks = model // LANE, other // LANE
    centre = centre[None, :]
    wide = (groups, 16, LANE)

    send, genotypes, cols = gather(groups, genotypes, imputed, centre, phenotypes, earlier, genetic, noise)
    got = exchange(send, "samp")
    owner = functools.partial(owner_kernel, float(rows * groups), model_blocks)
    send, keep = call(owner, [(wide, BF16, 0), ((4, pheno, LANE), F32, 0)], got, cols)
    got = exchange(send, "samp")
    back0 = functools.partial(back0_kernel, model_blocks, other_blocks)
    outs = [((ways, 16, rows // 2), BF16, 0), ((pheno, rows), F32, 0), ((1, model), F32, 0), ((pheno, other), F32, 1)]
    send, start, mean, scores = call(back0, outs, got, genotypes, centre, phenotypes, keep)
    got = exchange(send, "var")
    project = functools.partial(project_kernel, model_blocks)
    send, image = call(project, [(wide, BF16, 0), ((pheno, rows), F32, 0)], got, genotypes, start, mean)
    got = exchange(send, "samp")
    send, coef = call(next_kernel, [(wide, BF16, 0), ((pheno, LANE), F32, 0)], got, keep, cols)
    got = exchange(send, "samp")
    back1 = functools.partial(back1_kernel, model_blocks)
    (send,) = call(back1, [((ways, pheno, LANE), F32, 0)], got, genotypes, mean)
    got = exchange(send, "var")
    part = (pheno, rows // ways)
    out, residual = call(finish_kernel, [(part, F32, 1), (part, F32, 1)], got, start, image, coef, cols)
    return (out, residual, scores)


def solution(mesh):
    in_specs = (
        P("samp", "var"),
        P("samp", "var"),
        P("samp"),
        P(None, "samp"),
        P(None, "samp"),
        P(),
        P(),
    )
    out_specs = (P(None, ("samp", "var")), P(None, ("samp", "var")), P(None, "var"))
    return jax.shard_map(shards, mesh=mesh, in_specs=in_specs, out_specs=out_specs, check_vma=False)
```

```python
import functools

import jax
import jax.numpy as jnp
from jax import lax
from jax.experimental import pallas as pl
from jax.experimental.pallas import tpu as pltpu
from jax.sharding import PartitionSpec as P

M = 40960
CENTRES = 22
SLOTS = 12
LANE = 128
BASE = 4096.0
STEPS = 5
GRANT = 16 << 20
NEAR, CORES = 4, 2
BF16, F32 = jnp.bfloat16, jnp.float32
NT = (((1,), (1,)), ((), ()))


def split(x, parts):
    out = []
    for _ in range(parts):
        top = x.astype(BF16)
        out.append(top)
        x = x - top.astype(F32)
    return out


def dot(x, y):
    return jnp.dot(x, y, preferred_element_type=F32)


def dot_t(x, y):
    return lax.dot_general(x, y, NT, preferred_element_type=F32)


def iota(shape, dim):
    return lax.broadcasted_iota(jnp.int32, shape, dim)


def row_sum(x):
    return jnp.sum(x, axis=1, keepdims=True)


def in_lanes(columns):
    lane = iota((columns[0].shape[0], LANE), 1)
    out = jnp.zeros((columns[0].shape[0], LANE), F32)
    for at, column in enumerate(columns):
        out = jnp.where(lane == at, column, out)
    return out


def cut(x, at):
    return x[:, at * LANE : (at + 1) * LANE]


def square_sum(ref, first, wide):
    acc = None
    for at in range(0, ref.shape[0], 16):
        part = ref[at : at + 16, first : first + wide]
        acc = part * part if acc is None else acc + part * part
    return jnp.sum(acc.astype(F32), axis=0, keepdims=True)


def gather_kernel(
    gen_hbm, imp_hbm, centre_hbm, phen_hbm, earl_hbm, genetic_hbm, noise_hbm,
    out_ref, gen_ref, cols_ref, imp_ref, centre_ref, phen_ref, earl_ref, scal_ref, sem,
):
    rows, model = gen_ref.shape
    groups, pheno = out_ref.shape[0], phen_ref.shape[0]
    wide, narrow = model // STEPS, imp_ref.shape[1] // STEPS
    own, other = wide // LANE, narrow // LANE
    first_other = own * STEPS
    small = [(centre_hbm, centre_ref), (phen_hbm, phen_ref), (earl_hbm, earl_ref)]
    small += [(genetic_hbm, scal_ref.at[0]), (noise_hbm, scal_ref.at[1])]
    copies = [pltpu.make_async_copy(x, y, sem.at[i]) for i, (x, y) in enumerate(small)]
    for step in range(STEPS):
        cols = pl.ds(step * wide, wide)
        copies.append(pltpu.make_async_copy(gen_hbm.at[:, cols], gen_ref.at[:, cols], sem.at[5 + 2 * step]))
        cols = pl.ds(step * narrow, narrow)
        copies.append(pltpu.make_async_copy(imp_hbm.at[:, cols], imp_ref.at[:, cols], sem.at[6 + 2 * step]))
    for copy in copies:
        copy.start()

    spot = iota((LANE, rows), 0)
    slot = iota((16, rows), 0)
    for copy in copies[:3]:
        copy.wait()
    centre = centre_ref[...]
    pairs = jnp.where(slot < SLOTS, jnp.where(centre == slot, 1.0, jnp.where(centre == slot + SLOTS, BASE, 0.0)), 0.0)
    pieces = [p.astype(F32) for p in split(phen_ref[...], 3)]
    phen = jnp.concatenate(pieces + [jnp.ones((pheno, rows), F32)], axis=0).astype(BF16)
    left = jnp.concatenate(pieces + [pairs], axis=0).astype(BF16)
    earl = earl_ref[...]
    pieces = [p.astype(F32) for p in split(earl, 3)]
    right = jnp.concatenate(pieces + [jnp.ones((pheno, rows), F32)], axis=0).astype(BF16)
    sums = []
    for at in (0, 32, 64):
        full = dot_t(phen, jnp.where(spot == centre + at, 1.0, 0.0).astype(BF16))
        sums.append(full[24:32] if at == 64 else full[0:8] + full[8:16] + full[16:24])
    row = iota((pheno, LANE), 0)
    table = jnp.where(row < 4, 0.0, pltpu.roll(sums[0], 4, 0) + sums[1] + sums[2])
    moments = in_lanes([row_sum(earl), row_sum(earl * earl)])
    for at in range(first_other + other * STEPS, groups):
        out_ref[at, 0:8, :] = jnp.zeros((8, LANE), F32)
        out_ref[at, 8:16, :] = jnp.zeros((8, LANE), F32)
        out_ref[at, 16:24, :] = table
    for copy in copies[3:5]:
        copy.wait()
    for at in range(2):
        column = jnp.zeros((pheno, LANE), F32)
        for k in range(pheno):
            column = jnp.where(row == k, scal_ref[at, k], column)
        cols_ref[at] = column * (1.0 / M) if at == 0 else column

    for step in range(STEPS):
        copies[5 + 2 * step].wait()
        gen = gen_ref[:, step * wide : (step + 1) * wide]
        full = dot(left, gen)
        by_model = full[0:8] + full[8:16] + full[16:24]
        packed, square = full[24:40], square_sum(gen_ref, step * wide, wide) * BASE
        for at in range(own):
            block = step * own + at
            out_ref[block, 0:8, :] = cut(by_model, at)
            out_ref[block, 8:16, :] = cut(packed[0:8], at)
            counts = cut(packed[8:16], at) + table
            out_ref[block, 16:24, :] = counts + jnp.where(row == CENTRES - SLOTS - 8, cut(square, at), 0.0)
        copies[6 + 2 * step].wait()
        imp = imp_ref[:, step * narrow : (step + 1) * narrow]
        full = dot(right, imp)
        by_other = full[0:8] + full[8:16] + full[16:24]
        square = square_sum(imp_ref, step * narrow, narrow)
        for at in range(other):
            block = first_other + step * other + at
            counts = jnp.where(row == 0, cut(full[24:32], at), jnp.where(row == 1, cut(square, at), table))
            out_ref[block, 0:8, :] = cut(by_other, at)
            out_ref[block, 8:16, :] = moments
            out_ref[block, 16:24, :] = counts


def gather(groups, *operands):
    genotypes, imputed, _, phenotypes = operands[:4]
    rows, model = genotypes.shape
    other = imputed.shape[1]
    pheno = phenotypes.shape[0]
    return pl.pallas_call(
        gather_kernel,
        out_shape=[
            pltpu.VMEM((groups, 24, LANE), F32),
            pltpu.VMEM((rows, model), BF16),
            pltpu.VMEM((2, pheno, LANE), F32),
        ],
        in_specs=[pl.BlockSpec(memory_space=pltpu.HBM)] * len(operands),
        out_specs=[pl.BlockSpec(memory_space=pltpu.VMEM)] * 3,
        scratch_shapes=[
            pltpu.VMEM((rows, other), BF16),
            pltpu.VMEM((1, rows), jnp.int32),
            pltpu.VMEM((pheno, rows), F32),
            pltpu.VMEM((pheno, rows), F32),
            pltpu.SMEM((2, pheno), F32),
            pltpu.SemaphoreType.DMA((5 + 2 * STEPS,)),
        ],
        compiler_params=pltpu.CompilerParams(vmem_limit_bytes=GRANT),
    )(*[pltpu.with_memory_space_constraint(x, pltpu.HBM) for x in operands])


def call(kernel, outs, *operands, make=pltpu.VMEM):
    return pl.pallas_call(
        kernel,
        out_shape=[make(shape, kind) for shape, kind in outs],
        in_specs=[pl.BlockSpec(memory_space=pltpu.VMEM)] * len(operands),
        out_specs=[pl.BlockSpec(memory_space=pltpu.VMEM)] * len(outs),
        compiler_params=pltpu.CompilerParams(vmem_limit_bytes=GRANT),
    )(*[pltpu.with_memory_space_constraint(x, pltpu.VMEM) for x in operands])


def owner_kernel(total, model_blocks, got_ref, cols_ref, send_ref, keep_ref):
    groups, pheno = got_ref.shape[0], 8
    got = got_ref[...]
    raw = jnp.sum(got, axis=0)
    pack = got[:, 8:24, :]
    high = jnp.floor(pack * (1.0 / BASE))
    low = jnp.sum(pack - BASE * high, axis=0)
    high = jnp.sum(high, axis=0)
    table = raw[16:24]
    row = iota((pheno, LANE), 0)
    lane = iota((pheno, LANE), 1)
    sums = jnp.where(row < 4, pltpu.roll(table, 4, 0), pltpu.roll(table, LANE - 32, 1))
    sums = jnp.where(lane < CENTRES, sums, 0.0)
    count = pltpu.roll(table, LANE - 64, 1)
    count = jnp.where(row < 4, pltpu.roll(count, 4, 0), count)
    count = jnp.where(lane < CENTRES, count, 0.0)
    centre_mean = sums / jnp.maximum(count, 1.0)
    left = row_sum(sums - centre_mean * count)
    proj = raw[0:8]
    seen = jnp.zeros((1, LANE), F32)
    for c in range(CENTRES):
        line = low[c : c + 1] if c < SLOTS else high[c - SLOTS : c - SLOTS + 1]
        seen = seen + line
        proj = proj - centre_mean[:, c : c + 1] * line
    mean = seen / total
    spread = high[CENTRES - SLOTS : CENTRES - SLOTS + 1] / total - mean * mean + 1e-05
    scale = lax.rsqrt(spread)
    proj = (proj - left * mean) * scale
    back = proj * scale * cols_ref[0]
    lines = jnp.zeros((pheno, LANE), F32)
    for at, line in enumerate(split(mean, 3) + split(scale * scale, 3) + split(spread, 2)):
        lines = jnp.where(row == at, line.astype(F32), lines)

    other_mean = raw[16:17] / total
    other_var = raw[17:18] / total - other_mean * other_mean + 1e-05
    moments = raw[8:16]
    earlier_var = moments[:, 1:2] / total + 1e-05
    score = (raw[0:8] - moments[:, 0:1] * other_mean) / jnp.sqrt(total * other_var * earlier_var)
    score_top = score.astype(BF16).astype(F32)

    owner = lax.axis_index("samp") < model_blocks
    send = jnp.concatenate([jnp.where(owner, back, score_top), jnp.where(owner, lines, score - score_top)], axis=0)
    send_ref[...] = jnp.broadcast_to(send.astype(BF16)[None], (groups, 16, LANE))
    keep_ref[...] = centre_mean


def back_product(got_ref, gen_ref, model_blocks):
    acc = None
    for at in range(0, model_blocks, 2):
        values = jnp.concatenate([got_ref[at], got_ref[at + 1]], axis=1)
        part = dot_t(values, gen_ref[:, at * LANE : (at + 2) * LANE])
        acc = part if acc is None else acc + part
    return acc[0:8]


def back0_kernel(
    model_blocks, other_blocks,
    got_ref, gen_ref, centre_ref, phen_ref, keep_ref, cols_ref,
    send_ref, part_ref, start_ref, mean_ref, weight_ref, back_ref, score_ref, own_ref,
):
    ways = send_ref.shape[0]
    pheno, rows = phen_ref.shape
    shift = jnp.zeros((pheno, LANE), F32)
    own = jnp.zeros((pheno, LANE), F32)
    for at in range(model_blocks):
        block = got_ref[at].astype(F32)
        cols = slice(at * LANE, (at + 1) * LANE)
        mean = block[8:9] + block[9:10] + block[10:11]
        mean_ref[:, cols] = mean
        weight_ref[:, cols] = block[11:12] + block[12:13] + block[13:14]
        back_ref[:, cols] = block[0:8]
        shift = shift + block[0:8] * mean
        own = own + block[0:8] * block[0:8] * (block[14:15] + block[15:16])
    acc = None
    for at in range(0, model_blocks, 2):
        values = jnp.concatenate([got_ref[at], got_ref[at + 1]], axis=1)
        part = dot_t(values, gen_ref[:, at * LANE : (at + 2) * LANE])
        acc = part if acc is None else acc + part
    part = acc[0:8] - row_sum(shift)
    part_ref[...] = part
    own_ref[...] = in_lanes([row_sum(own) / cols_ref[0][:, 0:1]])
    half = rows // 2
    send = jnp.concatenate([part[:, :half], part[:, half:]], axis=0).astype(BF16)
    send_ref[...] = jnp.broadcast_to(send[None], (ways, 16, half))
    for at in range(other_blocks):
        block = got_ref[model_blocks + at].astype(F32)
        score_ref[:, at * LANE : (at + 1) * LANE] = block[0:8] + block[8:16]
    centre = centre_ref[...]
    start = phen_ref[...]
    centre_mean = keep_ref[...]
    for c in range(CENTRES):
        start = start - jnp.where(centre == c, centre_mean[:, c : c + 1], 0.0)
    start_ref[...] = start


def thirds(columns):
    return in_lanes([p.astype(F32) for x in columns for p in split(x, 3)])


def from_thirds(x, count):
    return [row_sum(x[:, 3 * at : 3 * at + 3]) for at in range(count)]


def project_kernel(got_ref, gen_ref, start_ref, mean_ref, send_ref, image_ref):
    peers = send_ref.shape[0]
    both = jnp.sum(got_ref[...].astype(F32), axis=0)
    image = jnp.concatenate([both[0:8], both[8:16]], axis=1)
    image_ref[...] = image
    start = start_ref[...]
    grams = thirds([row_sum(x) for x in (start * start, start * image, image * image)])
    total = row_sum(image)
    left = jnp.concatenate([p.astype(F32) for p in split(image, 2)], axis=0).astype(BF16)
    half = gen_ref.shape[1] // 2
    for at in range(0, half, 2 * LANE):
        parts = []
        for first in (at, at + half):
            cols = slice(first, first + 2 * LANE)
            full = dot(left, gen_ref[:, cols])
            parts.append(full[0:8] + full[8:16] - total * mean_ref[:, cols])
        send = jnp.concatenate(parts, axis=0).astype(BF16)
        for peer in range(peers):
            send_ref[peer, :, at : at + 2 * LANE] = send
    send = jnp.concatenate([grams, jnp.zeros_like(grams)], axis=0).astype(BF16)
    for peer in range(peers):
        send_ref[peer, :, half : half + LANE] = send


def middle_kernel(got_ref, send_ref):
    peers, _, wide = send_ref.shape
    half = wide - LANE
    got = jnp.sum(got_ref[...].astype(F32), axis=0)
    grams = thirds(from_thirds(got[0:8, half:], 3))
    tail = jnp.concatenate([grams, jnp.zeros_like(grams)], axis=0)
    send = jnp.concatenate([got[:, :half], tail], axis=1).astype(BF16)
    send_ref[...] = jnp.broadcast_to(send[None], send_ref.shape)


def back1_kernel(
    got_ref, gen_ref, mean_ref, weight_ref, back_ref, part_ref, own_ref, cols_ref, send_ref, coef_ref
):
    ways, pheno, _ = send_ref.shape
    rows, model = gen_ref.shape
    half = model // 2
    wide = 2 * LANE
    genetic, noise = cols_ref[0][:, 0:1], cols_ref[1][:, 0:1]
    shift = jnp.zeros((pheno, wide), F32)
    new = jnp.zeros((pheno, wide), F32)
    mixed = jnp.zeros((pheno, wide), F32)
    acc = None
    for at in range(0, half, wide):
        got = jnp.sum(got_ref[:, :, at : at + wide].astype(F32), axis=0)
        for proj, first in ((got[0:8], at), (got[8:16], at + half)):
            cols = slice(first, first + wide)
            back = proj * weight_ref[:, cols] * genetic
            new = new + proj * back
            mixed = mixed + proj * back_ref[:, cols]
            shift = shift + back * mean_ref[:, cols]
            low = jnp.concatenate([p.astype(F32) for p in split(back, 2)], axis=0).astype(BF16)
            part = dot_t(low, gen_ref[:, cols])
            acc = part if acc is None else acc + part
    grams = jnp.sum(got_ref[:, :, half:].astype(F32), axis=0)
    norm0, cross, square = from_thirds(grams[0:8], 3)
    rate = cross / norm0
    alpha0 = 1.0 / (rate + noise)
    norm1 = alpha0 * alpha0 * (square - rate * cross)
    on_image, on_start = -alpha0, alpha0 * rate + norm1 / norm0
    length = on_image * on_image * square + 2.0 * on_image * on_start * cross + on_start * on_start * norm0
    coef_ref[...] = in_lanes([rate, alpha0, norm1, on_image, on_start, length])
    part = on_image * (acc[0:8] + acc[8:16] - row_sum(shift)) + on_start * part_ref[...]
    energy = on_image * on_image * row_sum(new) + on_start * on_start * own_ref[...][:, 0:1]
    energy = energy + 2.0 * on_image * on_start * row_sum(mixed)
    width = rows // ways
    per = LANE // width
    lane = iota((pheno, LANE), 1)
    for peer in range(ways):
        spot = (width * (peer % per) + width) % LANE
        send_ref[peer] = jnp.where(lane == spot, energy, cut(part, peer // per))


def finish_kernel(got_ref, start_ref, image_ref, coef_ref, cols_ref, out_ref, residual_ref):
    ways, pheno, _ = got_ref.shape
    rows = start_ref.shape[1]
    width = rows // ways
    per = LANE // width
    mine = lax.axis_index("var")
    tile, at = lax.div(mine, per), lax.rem(mine, per)
    got = jnp.sum(got_ref[...], axis=0)
    lane = iota((pheno, LANE), 1)
    curve = row_sum(jnp.where(lane == lax.rem(at * width + width, LANE), got, 0.0))
    start = jnp.zeros((pheno, LANE), F32)
    image = jnp.zeros((pheno, LANE), F32)
    for t in range(rows // LANE):
        start = jnp.where(tile == t, cut(start_ref[...], t), start)
        image = jnp.where(tile == t, cut(image_ref[...], t), image)
    coef, noise = coef_ref[...], cols_ref[1]
    rate, alpha0, norm1, on_image, on_start, length = [coef[:, i : i + 1] for i in range(6)]
    alpha1 = norm1 / (curve + noise * length)
    direction = on_image * image + on_start * start
    residual = -alpha0 * (image - rate * start) - alpha1 * (got + noise * direction)
    answer = alpha0 * start + alpha1 * direction
    out, left = answer[:, :width], residual[:, :width]
    for a in range(1, per):
        out = jnp.where(at == a, answer[:, a * width : (a + 1) * width], out)
        left = jnp.where(at == a, residual[:, a * width : (a + 1) * width], left)
    out_ref[...] = out
    residual_ref[...] = left


def exchange(x, axis, sets=None):
    return lax.all_to_all(x, axis, 0, 0, axis_index_groups=sets, tiled=True)


def shards(genotypes, imputed, centre, phenotypes, earlier, genetic, noise):
    rows, model = genotypes.shape
    other = imputed.shape[1]
    pheno = phenotypes.shape[0]
    groups, ways = lax.axis_size("samp"), lax.axis_size("var")
    model_blocks, other_blocks = model // LANE, other // LANE
    centre = centre[None, :]
    along = groups // (NEAR * CORES)
    at = lambda x, y, core: (x * NEAR + y) * CORES + core
    planes = [[at(x, y, core) for x in range(along) for core in range(CORES)] for y in range(NEAR)]
    lines = [[at(x, y, core) for y in range(NEAR)] for x in range(along) for core in range(CORES)]
    half = (16, model // 2 + LANE)

    send, genotypes, cols = gather(groups, genotypes, imputed, centre, phenotypes, earlier, genetic, noise)
    got = exchange(send, "samp")
    owner = functools.partial(owner_kernel, float(rows * groups), model_blocks)
    send, keep = call(owner, [((groups, 16, LANE), BF16), ((pheno, LANE), F32)], got, cols)
    got = exchange(send, "samp")
    back0 = functools.partial(back0_kernel, model_blocks, other_blocks)
    row, wide = ((1, model), F32), ((pheno, rows), F32)
    outs = [((ways, 16, rows // 2), BF16), wide, wide, row, row]
    outs += [((pheno, model), F32), ((pheno, other), F32), ((pheno, LANE), F32)]
    outs = call(back0, outs, got, genotypes, centre, phenotypes, keep, cols)
    send, part, start, mean, weight, back, scores, own = outs
    got = exchange(send, "var")
    outs = [((along * CORES,) + half, BF16), ((pheno, rows), F32)]
    send, image = call(project_kernel, outs, got, genotypes, start, mean)
    (send,) = call(middle_kernel, [((NEAR,) + half, BF16)], exchange(send, "samp", planes))
    got = exchange(send, "samp", lines)
    outs = [((ways, pheno, LANE), F32), ((pheno, LANE), F32)]
    send, coef = call(back1_kernel, outs, got, genotypes, mean, weight, back, part, own, cols)
    got = exchange(send, "var")
    part = ((pheno, rows // ways), F32)
    out, residual = call(finish_kernel, [part, part], got, start, image, coef, cols, make=jax.ShapeDtypeStruct)
    return (out, residual, scores)


def solution(mesh):
    in_specs = (
        P("samp", "var"),
        P("samp", "var"),
        P("samp"),
        P(None, "samp"),
        P(None, "samp"),
        P(),
        P(),
    )
    out_specs = (P(None, ("samp", "var")), P(None, ("samp", "var")), P(None, "var"))
    return jax.shard_map(shards, mesh=mesh, in_specs=in_specs, out_specs=out_specs, check_vma=False)
```

```python
import functools

import jax
import jax.numpy as jnp
from jax import lax
from jax.experimental import pallas as pl
from jax.experimental.pallas import tpu as pltpu
from jax.sharding import PartitionSpec as P

M = 40960
CENTRES = 22
SLOTS = 12
LANE = 128
BASE = 4096.0
STEPS = 2
GRANT = 16 << 20
NEAR, CORES = 4, 2
BF16, F32 = jnp.bfloat16, jnp.float32
NT = (((1,), (1,)), ((), ()))


def split(x, parts):
    out = []
    for _ in range(parts):
        top = x.astype(BF16)
        out.append(top)
        x = x - top.astype(F32)
    return out


def dot(x, y):
    return jnp.dot(x, y, preferred_element_type=F32)


def dot_t(x, y):
    return lax.dot_general(x, y, NT, preferred_element_type=F32)


def iota(shape, dim):
    return lax.broadcasted_iota(jnp.int32, shape, dim)


def row_sum(x):
    return jnp.sum(x, axis=1, keepdims=True)


def in_lanes(columns):
    lane = iota((columns[0].shape[0], LANE), 1)
    out = jnp.zeros((columns[0].shape[0], LANE), F32)
    for at, column in enumerate(columns):
        out = jnp.where(lane == at, column, out)
    return out


def cut(x, at):
    return x[:, at * LANE : (at + 1) * LANE]


def square_sum(ref, top, deep, first, wide):
    acc = None
    for at in range(top, top + deep, 16):
        part = ref[at : at + 16, first : first + wide]
        acc = part * part if acc is None else acc + part * part
    return jnp.sum(acc.astype(F32), axis=0, keepdims=True)


def gather_kernel(
    gen_hbm, imp_hbm, centre_hbm, phen_hbm, earl_hbm, genetic_hbm, noise_hbm,
    out_ref, gen_ref, cols_ref, imp_ref, centre_ref, phen_ref, earl_ref, scal_ref, left_ref, right_ref, sem,
):
    rows, model = gen_ref.shape
    groups, pheno = out_ref.shape[0], phen_ref.shape[0]
    extra = imp_ref.shape[1]
    deep, wide = rows // STEPS, 2 * LANE
    model_blocks, other_blocks = model // LANE, extra // LANE
    small = [(centre_hbm, centre_ref), (phen_hbm, phen_ref), (earl_hbm, earl_ref)]
    small += [(genetic_hbm, scal_ref.at[0]), (noise_hbm, scal_ref.at[1])]
    copies = [pltpu.make_async_copy(x, y, sem.at[i]) for i, (x, y) in enumerate(small)]
    for step in range(STEPS):
        part = pl.ds(step * deep, deep)
        copies.append(pltpu.make_async_copy(gen_hbm.at[part], gen_ref.at[part], sem.at[5 + 2 * step]))
        copies.append(pltpu.make_async_copy(imp_hbm.at[part], imp_ref.at[part], sem.at[6 + 2 * step]))
    for copy in copies:
        copy.start()

    spot = iota((LANE, rows), 0)
    slot = iota((16, rows), 0)
    for copy in copies[:3]:
        copy.wait()
    centre = centre_ref[...]
    pairs = jnp.where(slot < SLOTS, jnp.where(centre == slot, 1.0, jnp.where(centre == slot + SLOTS, BASE, 0.0)), 0.0)
    pieces = [p.astype(F32) for p in split(phen_ref[...], 3)]
    phen = jnp.concatenate(pieces + [jnp.ones((pheno, rows), F32)], axis=0).astype(BF16)
    left_ref[...] = jnp.concatenate(pieces + [pairs], axis=0).astype(BF16)
    earl = earl_ref[...]
    pieces = [p.astype(F32) for p in split(earl, 3)]
    right_ref[...] = jnp.concatenate(pieces + [jnp.ones((pheno, rows), F32)], axis=0).astype(BF16)
    sums = []
    for at in (0, 32, 64):
        full = dot_t(phen, jnp.where(spot == centre + at, 1.0, 0.0).astype(BF16))
        sums.append(full[24:32] if at == 64 else full[0:8] + full[8:16] + full[16:24])
    row = iota((pheno, LANE), 0)
    table = jnp.where(row < 4, 0.0, pltpu.roll(sums[0], 4, 0) + sums[1] + sums[2])
    moments = in_lanes([row_sum(earl), row_sum(earl * earl)])
    for at in range(model_blocks + other_blocks, groups):
        out_ref[at, 0:8, :] = jnp.zeros((8, LANE), F32)
        out_ref[at, 8:16, :] = jnp.zeros((8, LANE), F32)
        out_ref[at, 16:24, :] = table
    for copy in copies[3:5]:
        copy.wait()
    for at in range(2):
        column = jnp.zeros((pheno, LANE), F32)
        for k in range(pheno):
            column = jnp.where(row == k, scal_ref[at, k], column)
        cols_ref[at] = column * (1.0 / M) if at == 0 else column

    for step in range(STEPS):
        top, last = step * deep, step == STEPS - 1
        copies[5 + 2 * step].wait()
        for first in range(0, model, wide):
            cols = slice(first, first + wide)
            full = dot(left_ref[:, top : top + deep], gen_ref[top : top + deep, cols])
            square = square_sum(gen_ref, top, deep, first, wide) * BASE
            by_model = full[0:8] + full[8:16] + full[16:24]
            tail = full[32:40] + jnp.where(iota((pheno, wide), 0) == CENTRES - SLOTS - 8, square, 0.0)
            for at in range(2):
                block = first // LANE + at
                for place, part in ((0, by_model), (8, full[24:32]), (16, tail)):
                    part = cut(part, at)
                    if step:
                        part = part + out_ref[block, place : place + 8, :]
                    if last and place == 16:
                        part = part + table
                    out_ref[block, place : place + 8, :] = part
        copies[6 + 2 * step].wait()
        for first in range(0, extra, wide):
            cols = slice(first, first + wide)
            full = dot(right_ref[:, top : top + deep], imp_ref[top : top + deep, cols])
            square = square_sum(imp_ref, top, deep, first, wide)
            by_other = full[0:8] + full[8:16] + full[16:24]
            lines = iota((pheno, wide), 0)
            counts = jnp.where(lines == 0, full[24:32], jnp.where(lines == 1, square, 0.0))
            for at in range(2):
                block = model_blocks + first // LANE + at
                for place, part in ((0, by_other), (16, counts)):
                    part = cut(part, at)
                    if step:
                        part = part + out_ref[block, place : place + 8, :]
                    if last and place == 16:
                        part = part + table
                    out_ref[block, place : place + 8, :] = part
                if last:
                    out_ref[block, 8:16, :] = moments


def gather(groups, *operands):
    genotypes, imputed, _, phenotypes = operands[:4]
    rows, model = genotypes.shape
    other = imputed.shape[1]
    pheno = phenotypes.shape[0]
    return pl.pallas_call(
        gather_kernel,
        out_shape=[
            pltpu.VMEM((groups, 24, LANE), F32),
            pltpu.VMEM((rows, model), BF16),
            pltpu.VMEM((2, pheno, LANE), F32),
        ],
        in_specs=[pl.BlockSpec(memory_space=pltpu.HBM)] * len(operands),
        out_specs=[pl.BlockSpec(memory_space=pltpu.VMEM)] * 3,
        scratch_shapes=[
            pltpu.VMEM((rows, other), BF16),
            pltpu.VMEM((1, rows), jnp.int32),
            pltpu.VMEM((pheno, rows), F32),
            pltpu.VMEM((pheno, rows), F32),
            pltpu.SMEM((2, pheno), F32),
            pltpu.VMEM((40, rows), BF16),
            pltpu.VMEM((32, rows), BF16),
            pltpu.SemaphoreType.DMA((5 + 2 * STEPS,)),
        ],
        compiler_params=pltpu.CompilerParams(vmem_limit_bytes=GRANT),
    )(*[pltpu.with_memory_space_constraint(x, pltpu.HBM) for x in operands])


def call(kernel, outs, *operands, make=pltpu.VMEM, out=None, scratch=()):
    out_shape = [make(shape, kind) for shape, kind in outs]
    out_specs = [pl.BlockSpec(memory_space=pltpu.VMEM)] * len(outs)
    if out is not None:
        out_shape.append(jax.ShapeDtypeStruct(*out))
        out_specs.append(pl.BlockSpec(memory_space=pltpu.HBM))
    return pl.pallas_call(
        kernel,
        out_shape=out_shape,
        in_specs=[pl.BlockSpec(memory_space=pltpu.VMEM)] * len(operands),
        out_specs=out_specs,
        scratch_shapes=scratch,
        compiler_params=pltpu.CompilerParams(vmem_limit_bytes=GRANT),
    )(*[pltpu.with_memory_space_constraint(x, pltpu.VMEM) for x in operands])


def owner_kernel(total, model_blocks, got_ref, cols_ref, send_ref, keep_ref):
    groups, pheno = got_ref.shape[0], 8
    got = got_ref[...]
    raw = jnp.sum(got, axis=0)
    pack = got[:, 8:24, :]
    high = jnp.floor(pack * (1.0 / BASE))
    low = jnp.sum(pack - BASE * high, axis=0)
    high = jnp.sum(high, axis=0)
    table = raw[16:24]
    row = iota((pheno, LANE), 0)
    lane = iota((pheno, LANE), 1)
    sums = jnp.where(row < 4, pltpu.roll(table, 4, 0), pltpu.roll(table, LANE - 32, 1))
    sums = jnp.where(lane < CENTRES, sums, 0.0)
    count = pltpu.roll(table, LANE - 64, 1)
    count = jnp.where(row < 4, pltpu.roll(count, 4, 0), count)
    count = jnp.where(lane < CENTRES, count, 0.0)
    centre_mean = sums / jnp.maximum(count, 1.0)
    left = row_sum(sums - centre_mean * count)
    proj = raw[0:8]
    seen = jnp.zeros((1, LANE), F32)
    for c in range(CENTRES):
        line = low[c : c + 1] if c < SLOTS else high[c - SLOTS : c - SLOTS + 1]
        seen = seen + line
        proj = proj - centre_mean[:, c : c + 1] * line
    mean = seen / total
    spread = high[CENTRES - SLOTS : CENTRES - SLOTS + 1] / total - mean * mean + 1e-05
    scale = lax.rsqrt(spread)
    proj = (proj - left * mean) * scale
    back = proj * scale * cols_ref[0]
    lines = jnp.zeros((pheno, LANE), F32)
    for at, line in enumerate(split(mean, 3) + split(scale * scale, 3) + split(spread, 2)):
        lines = jnp.where(row == at, line.astype(F32), lines)

    other_mean = raw[16:17] / total
    other_var = raw[17:18] / total - other_mean * other_mean + 1e-05
    moments = raw[8:16]
    earlier_var = moments[:, 1:2] / total + 1e-05
    score = (raw[0:8] - moments[:, 0:1] * other_mean) / jnp.sqrt(total * other_var * earlier_var)
    score_top = score.astype(BF16).astype(F32)

    owner = lax.axis_index("samp") < model_blocks
    send = jnp.concatenate([jnp.where(owner, back, score_top), jnp.where(owner, lines, score - score_top)], axis=0)
    send_ref[...] = jnp.broadcast_to(send.astype(BF16)[None], (groups, 16, LANE))
    keep_ref[...] = centre_mean


def back_product(got_ref, gen_ref, model_blocks):
    acc = None
    for at in range(0, model_blocks, 2):
        values = jnp.concatenate([got_ref[at], got_ref[at + 1]], axis=1)
        part = dot_t(values, gen_ref[:, at * LANE : (at + 2) * LANE])
        acc = part if acc is None else acc + part
    return acc[0:8]


def back0_kernel(
    model_blocks, other_blocks,
    got_ref, gen_ref, centre_ref, phen_ref, keep_ref, cols_ref,
    send_ref, part_ref, start_ref, mean_ref, weight_ref, back_ref, score_ref, own_ref,
):
    ways = send_ref.shape[0]
    pheno, rows = phen_ref.shape
    shift = jnp.zeros((pheno, LANE), F32)
    own = jnp.zeros((pheno, LANE), F32)
    for at in range(model_blocks):
        block = got_ref[at].astype(F32)
        cols = slice(at * LANE, (at + 1) * LANE)
        mean = block[8:9] + block[9:10] + block[10:11]
        mean_ref[:, cols] = mean
        weight_ref[:, cols] = block[11:12] + block[12:13] + block[13:14]
        back_ref[:, cols] = block[0:8]
        shift = shift + block[0:8] * mean
        own = own + block[0:8] * block[0:8] * (block[14:15] + block[15:16])
    acc = None
    for at in range(0, model_blocks, 2):
        values = jnp.concatenate([got_ref[at], got_ref[at + 1]], axis=1)
        part = dot_t(values, gen_ref[:, at * LANE : (at + 2) * LANE])
        acc = part if acc is None else acc + part
    part = acc[0:8] - row_sum(shift)
    part_ref[...] = part
    own_ref[...] = in_lanes([row_sum(own) / cols_ref[0][:, 0:1]])
    half = rows // 2
    send = jnp.concatenate([part[:, :half], part[:, half:]], axis=0).astype(BF16)
    send_ref[...] = jnp.broadcast_to(send[None], (ways, 16, half))
    for at in range(other_blocks):
        block = got_ref[model_blocks + at].astype(F32)
        score_ref[:, at * LANE : (at + 1) * LANE] = block[0:8] + block[8:16]
    centre = centre_ref[...]
    start = phen_ref[...]
    centre_mean = keep_ref[...]
    for c in range(CENTRES):
        start = start - jnp.where(centre == c, centre_mean[:, c : c + 1], 0.0)
    start_ref[...] = start


def thirds(columns):
    return in_lanes([p.astype(F32) for x in columns for p in split(x, 3)])


def from_thirds(x, count):
    return [row_sum(x[:, 3 * at : 3 * at + 3]) for at in range(count)]


def project_kernel(got_ref, gen_ref, start_ref, mean_ref, send_ref, image_ref):
    peers = send_ref.shape[0]
    both = jnp.sum(got_ref[...].astype(F32), axis=0)
    image = jnp.concatenate([both[0:8], both[8:16]], axis=1)
    image_ref[...] = image
    start = start_ref[...]
    grams = thirds([row_sum(x) for x in (start * start, start * image, image * image)])
    total = row_sum(image)
    left = jnp.concatenate([p.astype(F32) for p in split(image, 2)], axis=0).astype(BF16)
    half = gen_ref.shape[1] // 2
    for at in range(0, half, 2 * LANE):
        parts = []
        for first in (at, at + half):
            cols = slice(first, first + 2 * LANE)
            full = dot(left, gen_ref[:, cols])
            parts.append(full[0:8] + full[8:16] - total * mean_ref[:, cols])
        send = jnp.concatenate(parts, axis=0).astype(BF16)
        for peer in range(peers):
            send_ref[peer, :, at : at + 2 * LANE] = send
    send = jnp.concatenate([grams, jnp.zeros_like(grams)], axis=0).astype(BF16)
    for peer in range(peers):
        send_ref[peer, :, half : half + LANE] = send


def middle_kernel(got_ref, send_ref):
    peers, _, wide = send_ref.shape
    half = wide - LANE
    got = jnp.sum(got_ref[...].astype(F32), axis=0)
    grams = thirds(from_thirds(got[0:8, half:], 3))
    tail = jnp.concatenate([grams, jnp.zeros_like(grams)], axis=0)
    send = jnp.concatenate([got[:, :half], tail], axis=1).astype(BF16)
    send_ref[...] = jnp.broadcast_to(send[None], send_ref.shape)


def back1_kernel(
    got_ref, gen_ref, mean_ref, weight_ref, back_ref, part_ref, own_ref, cols_ref, score_ref,
    send_ref, coef_ref, out_hbm, sem,
):
    copy = pltpu.make_async_copy(score_ref, out_hbm, sem)
    copy.start()
    ways, pheno, _ = send_ref.shape
    rows, model = gen_ref.shape
    half = model // 2
    wide = 2 * LANE
    genetic, noise = cols_ref[0][:, 0:1], cols_ref[1][:, 0:1]
    shift = jnp.zeros((pheno, wide), F32)
    new = jnp.zeros((pheno, wide), F32)
    mixed = jnp.zeros((pheno, wide), F32)
    acc = None
    for at in range(0, half, wide):
        got = jnp.sum(got_ref[:, :, at : at + wide].astype(F32), axis=0)
        for proj, first in ((got[0:8], at), (got[8:16], at + half)):
            cols = slice(first, first + wide)
            back = proj * weight_ref[:, cols] * genetic
            new = new + proj * back
            mixed = mixed + proj * back_ref[:, cols]
            shift = shift + back * mean_ref[:, cols]
            low = jnp.concatenate([p.astype(F32) for p in split(back, 2)], axis=0).astype(BF16)
            part = dot_t(low, gen_ref[:, cols])
            acc = part if acc is None else acc + part
    grams = jnp.sum(got_ref[:, :, half:].astype(F32), axis=0)
    norm0, cross, square = from_thirds(grams[0:8], 3)
    rate = cross / norm0
    alpha0 = 1.0 / (rate + noise)
    norm1 = alpha0 * alpha0 * (square - rate * cross)
    on_image, on_start = -alpha0, alpha0 * rate + norm1 / norm0
    length = on_image * on_image * square + 2.0 * on_image * on_start * cross + on_start * on_start * norm0
    coef_ref[...] = in_lanes([rate, alpha0, norm1, on_image, on_start, length])
    part = on_image * (acc[0:8] + acc[8:16] - row_sum(shift)) + on_start * part_ref[...]
    energy = on_image * on_image * row_sum(new) + on_start * on_start * own_ref[...][:, 0:1]
    energy = energy + 2.0 * on_image * on_start * row_sum(mixed)
    width = rows // ways
    per = LANE // width
    lane = iota((pheno, LANE), 1)
    for peer in range(ways):
        spot = (width * (peer % per) + width) % LANE
        send_ref[peer] = jnp.where(lane == spot, energy, cut(part, peer // per))
    copy.wait()


def finish_kernel(got_ref, start_ref, image_ref, coef_ref, cols_ref, out_ref, residual_ref):
    ways, pheno, _ = got_ref.shape
    rows = start_ref.shape[1]
    width = rows // ways
    per = LANE // width
    mine = lax.axis_index("var")
    tile, at = lax.div(mine, per), lax.rem(mine, per)
    got = jnp.sum(got_ref[...], axis=0)
    lane = iota((pheno, LANE), 1)
    curve = row_sum(jnp.where(lane == lax.rem(at * width + width, LANE), got, 0.0))
    start = jnp.zeros((pheno, LANE), F32)
    image = jnp.zeros((pheno, LANE), F32)
    for t in range(rows // LANE):
        start = jnp.where(tile == t, cut(start_ref[...], t), start)
        image = jnp.where(tile == t, cut(image_ref[...], t), image)
    coef, noise = coef_ref[...], cols_ref[1]
    rate, alpha0, norm1, on_image, on_start, length = [coef[:, i : i + 1] for i in range(6)]
    alpha1 = norm1 / (curve + noise * length)
    direction = on_image * image + on_start * start
    residual = -alpha0 * (image - rate * start) - alpha1 * (got + noise * direction)
    answer = alpha0 * start + alpha1 * direction
    out, left = answer[:, :width], residual[:, :width]
    for a in range(1, per):
        out = jnp.where(at == a, answer[:, a * width : (a + 1) * width], out)
        left = jnp.where(at == a, residual[:, a * width : (a + 1) * width], left)
    out_ref[...] = out
    residual_ref[...] = left


def exchange(x, axis, sets=None):
    return lax.all_to_all(x, axis, 0, 0, axis_index_groups=sets, tiled=True)


def shards(genotypes, imputed, centre, phenotypes, earlier, genetic, noise):
    rows, model = genotypes.shape
    other = imputed.shape[1]
    pheno = phenotypes.shape[0]
    groups, ways = lax.axis_size("samp"), lax.axis_size("var")
    model_blocks, other_blocks = model // LANE, other // LANE
    centre = centre[None, :]
    along = groups // (NEAR * CORES)
    at = lambda x, y, core: (x * NEAR + y) * CORES + core
    planes = [[at(x, y, core) for x in range(along) for core in range(CORES)] for y in range(NEAR)]
    lines = [[at(x, y, core) for y in range(NEAR)] for x in range(along) for core in range(CORES)]
    half = (16, model // 2 + LANE)

    send, genotypes, cols = gather(groups, genotypes, imputed, centre, phenotypes, earlier, genetic, noise)
    got = exchange(send, "samp")
    owner = functools.partial(owner_kernel, float(rows * groups), model_blocks)
    send, keep = call(owner, [((groups, 16, LANE), BF16), ((pheno, LANE), F32)], got, cols)
    got = exchange(send, "samp")
    back0 = functools.partial(back0_kernel, model_blocks, other_blocks)
    row, wide = ((1, model), F32), ((pheno, rows), F32)
    outs = [((ways, 16, rows // 2), BF16), wide, wide, row, row]
    outs += [((pheno, model), F32), ((pheno, other), F32), ((pheno, LANE), F32)]
    outs = call(back0, outs, got, genotypes, centre, phenotypes, keep, cols)
    send, part, start, mean, weight, back, scores, own = outs
    got = exchange(send, "var")
    outs = [((along * CORES,) + half, BF16), ((pheno, rows), F32)]
    send, image = call(project_kernel, outs, got, genotypes, start, mean)
    (send,) = call(middle_kernel, [((NEAR,) + half, BF16)], exchange(send, "samp", planes))
    got = exchange(send, "samp", lines)
    outs = [((ways, pheno, LANE), F32), ((pheno, LANE), F32)]
    kept = (got, genotypes, mean, weight, back, part, own, cols, scores)
    out, sem = ((pheno, other), F32), (pltpu.SemaphoreType.DMA,)
    send, coef, scores = call(back1_kernel, outs, *kept, out=out, scratch=sem)
    got = exchange(send, "var")
    part = ((pheno, rows // ways), F32)
    out, residual = call(finish_kernel, [part, part], got, start, image, coef, cols, make=jax.ShapeDtypeStruct)
    return (out, residual, scores)


def solution(mesh):
    in_specs = (
        P("samp", "var"),
        P("samp", "var"),
        P("samp"),
        P(None, "samp"),
        P(None, "samp"),
        P(),
        P(),
    )
    out_specs = (P(None, ("samp", "var")), P(None, ("samp", "var")), P(None, "var"))
    return jax.shard_map(shards, mesh=mesh, in_specs=in_specs, out_specs=out_specs, check_vma=False)
```

```python
import functools

import jax
import jax.numpy as jnp
from jax import lax
from jax.experimental import pallas as pl
from jax.experimental.pallas import tpu as pltpu
from jax.sharding import PartitionSpec as P

M = 40960
CENTRES = 22
SLOTS = 12
LANE = 128
BASE = 4096.0
STEPS = 2
GRANT = 16 << 20
NEAR, CORES = 4, 2
BF16, F32 = jnp.bfloat16, jnp.float32
NT = (((1,), (1,)), ((), ()))


def split(x, parts):
    out = []
    for _ in range(parts):
        top = x.astype(BF16)
        out.append(top)
        x = x - top.astype(F32)
    return out


def dot(x, y):
    return jnp.dot(x, y, preferred_element_type=F32)


def dot_t(x, y):
    return lax.dot_general(x, y, NT, preferred_element_type=F32)


def iota(shape, dim):
    return lax.broadcasted_iota(jnp.int32, shape, dim)


def row_sum(x):
    return jnp.sum(x, axis=1, keepdims=True)


def in_lanes(columns):
    lane = iota((columns[0].shape[0], LANE), 1)
    out = jnp.zeros((columns[0].shape[0], LANE), F32)
    for at, column in enumerate(columns):
        out = jnp.where(lane == at, column, out)
    return out


def cut(x, at):
    return x[:, at * LANE : (at + 1) * LANE]


def square_sum(ref, top, deep, first, wide):
    acc = None
    for at in range(top, top + deep, 16):
        part = ref[at : at + 16, first : first + wide]
        acc = part * part if acc is None else acc + part * part
    return jnp.sum(acc.astype(F32), axis=0, keepdims=True)


def gather_kernel(
    gen_hbm, imp_hbm, centre_hbm, phen_hbm, earl_hbm, genetic_hbm, noise_hbm,
    out_ref, gen_ref, cols_ref, imp_ref, centre_ref, phen_ref, earl_ref, scal_ref, left_ref, right_ref, model_ref, other_ref, sem,
):
    rows, model = gen_ref.shape
    groups, pheno = out_ref.shape[0], phen_ref.shape[0]
    extra = imp_ref.shape[1]
    deep, wide = rows // STEPS, 2 * LANE
    span, side = model // groups, extra // groups
    small = [(centre_hbm, centre_ref), (phen_hbm, phen_ref), (earl_hbm, earl_ref)]
    small += [(genetic_hbm, scal_ref.at[0]), (noise_hbm, scal_ref.at[1])]
    copies = [pltpu.make_async_copy(x, y, sem.at[i]) for i, (x, y) in enumerate(small)]
    for step in range(STEPS):
        part = pl.ds(step * deep, deep)
        copies.append(pltpu.make_async_copy(gen_hbm.at[part], gen_ref.at[part], sem.at[5 + 2 * step]))
        copies.append(pltpu.make_async_copy(imp_hbm.at[part], imp_ref.at[part], sem.at[6 + 2 * step]))
    for copy in copies:
        copy.start()

    spot = iota((LANE, rows), 0)
    slot = iota((16, rows), 0)
    for copy in copies[:3]:
        copy.wait()
    centre = centre_ref[...]
    pairs = jnp.where(slot < SLOTS, jnp.where(centre == slot, 1.0, jnp.where(centre == slot + SLOTS, BASE, 0.0)), 0.0)
    pieces = [p.astype(F32) for p in split(phen_ref[...], 3)]
    phen = jnp.concatenate(pieces + [jnp.ones((pheno, rows), F32)], axis=0).astype(BF16)
    left_ref[...] = jnp.concatenate(pieces + [pairs], axis=0).astype(BF16)
    earl = earl_ref[...]
    pieces = [p.astype(F32) for p in split(earl, 3)]
    right_ref[...] = jnp.concatenate(pieces + [jnp.ones((pheno, rows), F32)], axis=0).astype(BF16)
    sums = []
    here = jnp.where(spot == centre, 1.0, 0.0).astype(BF16)
    full = dot_t(phen, here)
    row, lane = iota((pheno, LANE), 0), iota((pheno, LANE), 1)
    sums, count = full[0:8] + full[8:16] + full[16:24], full[24:32]
    own_mean = sums / jnp.maximum(count, 1.0)
    full = dot(jnp.concatenate([p.astype(F32) for p in split(own_mean, 3)], axis=0).astype(BF16), here)
    apart = phen_ref[...] - (full[0:8] + full[8:16] + full[16:24])
    within = row_sum(apart * apart)
    table = pltpu.roll(sums, span, 1) + pltpu.roll(count, span + CENTRES, 1)
    table = table + pltpu.roll(in_lanes([within, row_sum(earl), row_sum(earl * earl)]), span + 2 * CENTRES, 1)
    for copy in copies[3:5]:
        copy.wait()
    for at in range(2):
        column = jnp.zeros((pheno, LANE), F32)
        for k in range(pheno):
            column = jnp.where(row == k, scal_ref[at, k], column)
        cols_ref[at] = column * (1.0 / M) if at == 0 else column

    for step in range(STEPS):
        top, last = step * deep, step == STEPS - 1
        copies[5 + 2 * step].wait()
        for first in range(0, model, wide):
            cols = slice(first, first + wide)
            full = dot(left_ref[:, top : top + deep], gen_ref[top : top + deep, cols])
            square = square_sum(gen_ref, top, deep, first, wide) * BASE
            tail = full[32:40] + jnp.where(iota((pheno, wide), 0) == CENTRES - SLOTS - 8, square, 0.0)
            for place, part in ((0, full[0:8] + full[8:16] + full[16:24]), (8, full[24:32]), (16, tail)):
                model_ref[place : place + 8, cols] = part + model_ref[place : place + 8, cols] if step else part
        copies[6 + 2 * step].wait()
        for first in range(0, extra, wide):
            cols = slice(first, first + wide)
            full = dot(right_ref[:, top : top + deep], imp_ref[top : top + deep, cols])
            square = square_sum(imp_ref, top, deep, first, wide)
            lines = iota((pheno, wide), 0)
            counts = jnp.where(lines == 0, full[24:32], jnp.where(lines == 1, square, 0.0))
            for place, part in ((0, full[0:8] + full[8:16] + full[16:24]), (8, counts)):
                other_ref[place : place + 8, cols] = part + other_ref[place : place + 8, cols] if step else part

    def window(ref, place, first, width, to):
        block, skip = divmod(first, LANE)
        turn = (to - skip) % LANE
        out = pltpu.roll(ref[place : place + 8, block * LANE : (block + 1) * LANE], turn, 1)
        if skip + width > LANE:
            more = pltpu.roll(ref[place : place + 8, (block + 1) * LANE : (block + 2) * LANE], turn, 1)
            out = jnp.where(lane < to + LANE - skip, out, more)
        return out

    for at in range(groups):
        mine = lambda place: window(model_ref, place, at * span, span, 0)
        more = lambda place: jnp.where(lane < span + side, window(other_ref, place, at * side, side, span), 0.0)
        top = jnp.where(lane < span, mine(0), more(0))
        centre_rows = jnp.where(lane < span, mine(8), table)
        tail = jnp.where(lane < span, mine(16), more(8))
        for place, part in enumerate((top[0:4], top[4:8], centre_rows[0:4], centre_rows[4:8], tail[0:4])):
            out_ref[at, :, place * LANE : (place + 1) * LANE] = part


def gather(groups, *operands):
    genotypes, imputed, _, phenotypes = operands[:4]
    rows, model = genotypes.shape
    other = imputed.shape[1]
    pheno = phenotypes.shape[0]
    return pl.pallas_call(
        gather_kernel,
        out_shape=[
            pltpu.VMEM((groups, 4, 5 * LANE), F32),
            pltpu.VMEM((rows, model), BF16),
            pltpu.VMEM((2, pheno, LANE), F32),
        ],
        in_specs=[pl.BlockSpec(memory_space=pltpu.HBM)] * len(operands),
        out_specs=[pl.BlockSpec(memory_space=pltpu.VMEM)] * 3,
        scratch_shapes=[
            pltpu.VMEM((rows, other), BF16),
            pltpu.VMEM((1, rows), jnp.int32),
            pltpu.VMEM((pheno, rows), F32),
            pltpu.VMEM((pheno, rows), F32),
            pltpu.SMEM((2, pheno), F32),
            pltpu.VMEM((40, rows), BF16),
            pltpu.VMEM((32, rows), BF16),
            pltpu.VMEM((24, model), F32),
            pltpu.VMEM((16, other), F32),
            pltpu.SemaphoreType.DMA((5 + 2 * STEPS,)),
        ],
        compiler_params=pltpu.CompilerParams(vmem_limit_bytes=GRANT),
    )(*[pltpu.with_memory_space_constraint(x, pltpu.HBM) for x in operands])


def call(kernel, outs, *operands, make=pltpu.VMEM, out=None, scratch=()):
    out_shape = [make(shape, kind) for shape, kind in outs]
    out_specs = [pl.BlockSpec(memory_space=pltpu.VMEM)] * len(outs)
    if out is not None:
        out_shape.append(jax.ShapeDtypeStruct(*out))
        out_specs.append(pl.BlockSpec(memory_space=pltpu.HBM))
    return pl.pallas_call(
        kernel,
        out_shape=out_shape,
        in_specs=[pl.BlockSpec(memory_space=pltpu.VMEM)] * len(operands),
        out_specs=out_specs,
        scratch_shapes=scratch,
        compiler_params=pltpu.CompilerParams(vmem_limit_bytes=GRANT),
    )(*[pltpu.with_memory_space_constraint(x, pltpu.VMEM) for x in operands])


def owner_kernel(total, span, side, got_ref, cols_ref, send_ref, keep_ref, norm_ref):
    groups, pheno = got_ref.shape[0], 8
    row, lane = iota((pheno, LANE), 0), iota((pheno, LANE), 1)
    pieces = [got_ref[:, :, at * LANE : (at + 1) * LANE] for at in range(5)]
    raw = [jnp.sum(x, axis=0) for x in pieces]
    tops = [jnp.floor(x * (1.0 / BASE)) for x in pieces[2:]]
    low = jnp.concatenate([jnp.sum(x - BASE * y, axis=0) for x, y in zip(pieces[2:], tops)], axis=0)
    high = jnp.concatenate([jnp.sum(y, axis=0) for y in tops], axis=0)
    product = jnp.concatenate(raw[0:2], axis=0)
    table = jnp.concatenate(raw[2:4], axis=0)
    sums = jnp.where(lane < CENTRES, pltpu.roll(table, LANE - span, 1), 0.0)
    count = jnp.where(lane < CENTRES, pltpu.roll(table, LANE - span - CENTRES, 1), 0.0)
    centre_mean = sums / jnp.maximum(count, 1.0)
    left = row_sum(sums - centre_mean * count)
    extra = span + 2 * CENTRES
    within, first, second = [table[:, extra + at : extra + at + 1] for at in range(3)]

    proj = product
    seen = jnp.zeros((1, LANE), F32)
    for c in range(CENTRES):
        line = low[c : c + 1] if c < SLOTS else high[c - SLOTS : c - SLOTS + 1]
        seen = seen + line
        proj = proj - centre_mean[:, c : c + 1] * line
    mean = seen / total
    spread = high[CENTRES - SLOTS : CENTRES - SLOTS + 1] / total - mean * mean + 1e-05
    scale = lax.rsqrt(spread)
    proj = (proj - left * mean) * scale
    back = proj * scale * cols_ref[0]
    lines = jnp.zeros((pheno, LANE), F32)
    for at, line in enumerate(split(mean, 3) + split(scale * scale, 3) + split(spread, 2)):
        lines = jnp.where(row == at, line.astype(F32), lines)

    other_mean = raw[4][0:1] / total
    other_var = raw[4][1:2] / total - other_mean * other_mean + 1e-05
    earlier_var = second / total + 1e-05
    score = (product - first * other_mean) / jnp.sqrt(total * other_var * earlier_var)
    score_top = score.astype(BF16).astype(F32)

    here, there = lane < span, lane < span + side
    top = jnp.where(here, back, jnp.where(there, score_top, 0.0))
    rest = jnp.where(here, lines, jnp.where(there, score - score_top, 0.0))
    send = jnp.concatenate([top, rest], axis=0).astype(BF16)
    send_ref[...] = jnp.broadcast_to(send[None], (groups, 16, LANE))
    keep_ref[...] = centre_mean

    middle = pltpu.roll(centre_mean, span, 1)
    halves = []
    for half in range(2):
        between = jnp.zeros((pheno // 2, LANE), F32)
        for at in range(groups):
            part = got_ref[at, :, (2 + half) * LANE : (3 + half) * LANE]
            counted = pltpu.roll(part, LANE - CENTRES, 1)
            apart = part - counted * middle[4 * half : 4 * half + 4]
            between = between + apart * apart / jnp.maximum(counted, 1.0)
        halves.append(between)
    between = jnp.concatenate(halves, axis=0)
    between = jnp.where((lane >= span) & (lane < span + CENTRES), between, 0.0)
    norm_ref[...] = jnp.broadcast_to(row_sum(between) + within, (pheno, LANE))


def back0_kernel(
    span, side, got_ref, gen_ref, centre_ref, phen_ref, keep_ref, cols_ref,
    send_ref, start_ref, mean_ref, weight_ref, back_ref, score_ref, own_ref,
):
    ways = send_ref.shape[0]
    pheno, rows = phen_ref.shape
    model, other = gen_ref.shape[1], score_ref.shape[1]

    def block_of(at, width, skip, rows, load):
        lane = iota((rows, LANE), 1)
        out = None
        for owner in range(at * LANE // width, ((at + 1) * LANE - 1) // width + 1):
            first = owner * width - at * LANE
            part = pltpu.roll(load(owner), (first - skip) % LANE, 1)
            out = part if out is None else jnp.where(lane < first, out, part)
        return out

    shift = jnp.zeros((pheno, LANE), F32)
    own = jnp.zeros((pheno, LANE), F32)
    acc = None
    for pair in range(0, model // LANE, 2):
        values = []
        for at in (pair, pair + 1):
            block = block_of(at, span, 0, 16, lambda owner: got_ref[owner].astype(F32))
            cols = slice(at * LANE, (at + 1) * LANE)
            mean = block[8:9] + block[9:10] + block[10:11]
            mean_ref[:, cols] = mean
            weight_ref[:, cols] = block[11:12] + block[12:13] + block[13:14]
            back_ref[:, cols] = block[0:8]
            shift = shift + block[0:8] * mean
            own = own + block[0:8] * block[0:8] * (block[14:15] + block[15:16])
            values.append(block.astype(BF16))
        part = dot_t(jnp.concatenate(values, axis=1), gen_ref[:, pair * LANE : (pair + 2) * LANE])
        acc = part if acc is None else acc + part
    part = acc[0:8] - row_sum(shift)
    own_ref[...] = in_lanes([row_sum(own) / cols_ref[0][:, 0:1]])
    half = rows // 2
    send = jnp.concatenate([part[:, :half], part[:, half:]], axis=0).astype(BF16)
    send_ref[...] = jnp.broadcast_to(send[None], (ways, 16, half))
    for at in range(other // LANE):
        load = lambda owner: got_ref[owner].astype(F32)[0:8] + got_ref[owner].astype(F32)[8:16]
        score_ref[:, at * LANE : (at + 1) * LANE] = block_of(at, side, span, pheno, load)
    centre = centre_ref[...]
    start = phen_ref[...]
    centre_mean = keep_ref[...]
    for c in range(CENTRES):
        start = start - jnp.where(centre == c, centre_mean[:, c : c + 1], 0.0)
    start_ref[...] = start


def project_kernel(got_ref, gen_ref, mean_ref, send_ref, image_ref):
    peers = send_ref.shape[0]
    both = jnp.sum(got_ref[...].astype(F32), axis=0)
    image = jnp.concatenate([both[0:8], both[8:16]], axis=1)
    image_ref[...] = image
    total = row_sum(image)
    left = jnp.concatenate([p.astype(F32) for p in split(image, 2)], axis=0).astype(BF16)
    half = gen_ref.shape[1] // 2
    for at in range(0, half, 2 * LANE):
        parts = []
        for first in (at, at + half):
            cols = slice(first, first + 2 * LANE)
            full = dot(left, gen_ref[:, cols])
            parts.append(full[0:8] + full[8:16] - total * mean_ref[:, cols])
        send = jnp.concatenate(parts, axis=0).astype(BF16)
        for peer in range(peers):
            send_ref[peer, :, at : at + 2 * LANE] = send


def middle_kernel(got_ref, send_ref):
    got = jnp.sum(got_ref[...].astype(F32), axis=0)
    send_ref[...] = jnp.broadcast_to(got.astype(BF16)[None], send_ref.shape)


def back1_kernel(
    got_ref, gen_ref, mean_ref, weight_ref, back_ref, own_ref, cols_ref, score_ref, send_ref, out_hbm, sem
):
    copy = pltpu.make_async_copy(score_ref, out_hbm, sem)
    copy.start()
    ways, pheno, _ = send_ref.shape
    rows, model = gen_ref.shape
    half = model // 2
    wide = 2 * LANE
    genetic = cols_ref[0][:, 0:1]
    shift = jnp.zeros((pheno, wide), F32)
    new = jnp.zeros((pheno, wide), F32)
    mixed = jnp.zeros((pheno, wide), F32)
    acc = None
    for at in range(0, half, wide):
        got = jnp.sum(got_ref[:, :, at : at + wide].astype(F32), axis=0)
        for proj, first in ((got[0:8], at), (got[8:16], at + half)):
            cols = slice(first, first + wide)
            back = proj * weight_ref[:, cols] * genetic
            new = new + proj * back
            mixed = mixed + proj * back_ref[:, cols]
            shift = shift + back * mean_ref[:, cols]
            low = jnp.concatenate([p.astype(F32) for p in split(back, 2)], axis=0).astype(BF16)
            part = dot_t(low, gen_ref[:, cols])
            acc = part if acc is None else acc + part
    part = acc[0:8] + acc[8:16] - row_sum(shift)
    energies = (own_ref[...][:, 0:1], row_sum(mixed), row_sum(new))
    width = rows // ways
    per = LANE // width
    lane = iota((pheno, LANE), 1)
    for peer in range(ways):
        send = cut(part, peer // per)
        for at, energy in enumerate(energies):
            send = jnp.where(lane == (width * (peer % per) + width + at) % LANE, energy, send)
        send_ref[peer] = send
    copy.wait()


def finish_kernel(got_ref, start_ref, image_ref, norm_ref, cols_ref, out_ref, residual_ref):
    ways, pheno, _ = got_ref.shape
    rows = start_ref.shape[1]
    width = rows // ways
    per = LANE // width
    mine = lax.axis_index("var")
    tile, at = lax.div(mine, per), lax.rem(mine, per)
    got = jnp.sum(got_ref[...], axis=0)
    lane = iota((pheno, LANE), 1)
    spots = [lax.rem(at * width + width + i, LANE) for i in range(3)]
    cross, square, cube = [row_sum(jnp.where(lane == spot, got, 0.0)) for spot in spots]
    norm0, noise = norm_ref[...][:, 0:1], cols_ref[1][:, 0:1]
    rate = cross / norm0
    alpha0 = 1.0 / (rate + noise)
    norm1 = alpha0 * alpha0 * (square - rate * cross)
    on_image, on_start = -alpha0, alpha0 * rate + norm1 / norm0
    both, first, last = on_image * on_image, 2.0 * on_image * on_start, on_start * on_start
    length = both * square + first * cross + last * norm0
    curve = both * cube + first * square + last * cross
    alpha1 = norm1 / (curve + noise * length)
    start = jnp.zeros((pheno, LANE), F32)
    image = jnp.zeros((pheno, LANE), F32)
    for t in range(rows // LANE):
        start = jnp.where(tile == t, cut(start_ref[...], t), start)
        image = jnp.where(tile == t, cut(image_ref[...], t), image)
    direction = on_image * image + on_start * start
    residual = -alpha0 * (image - rate * start) - alpha1 * (on_image * got + on_start * image + noise * direction)
    answer = alpha0 * start + alpha1 * direction
    out, left = answer[:, :width], residual[:, :width]
    for a in range(1, per):
        out = jnp.where(at == a, answer[:, a * width : (a + 1) * width], out)
        left = jnp.where(at == a, residual[:, a * width : (a + 1) * width], left)
    out_ref[...] = out
    residual_ref[...] = left


def exchange(x, axis, sets=None):
    return lax.all_to_all(x, axis, 0, 0, axis_index_groups=sets, tiled=True)


def shards(genotypes, imputed, centre, phenotypes, earlier, genetic, noise):
    rows, model = genotypes.shape
    other = imputed.shape[1]
    pheno = phenotypes.shape[0]
    groups, ways = lax.axis_size("samp"), lax.axis_size("var")
    span, side = model // groups, other // groups
    centre = centre[None, :]
    along = groups // (NEAR * CORES)
    at = lambda x, y, core: (x * NEAR + y) * CORES + core
    planes = [[at(x, y, core) for x in range(along) for core in range(CORES)] for y in range(NEAR)]
    lines = [[at(x, y, core) for y in range(NEAR)] for x in range(along) for core in range(CORES)]
    half = (16, model // 2)

    send, genotypes, cols = gather(groups, genotypes, imputed, centre, phenotypes, earlier, genetic, noise)
    got = exchange(send, "samp")
    owner = functools.partial(owner_kernel, float(rows * groups), span, side)
    tile = ((pheno, LANE), F32)
    send, keep, norm = call(owner, [((groups, 16, LANE), BF16), tile, tile], got, cols)
    got = exchange(send, "samp")
    back0 = functools.partial(back0_kernel, span, side)
    row, wide = ((1, model), F32), ((pheno, rows), F32)
    outs = [((ways, 16, rows // 2), BF16), wide, row, row]
    outs += [((pheno, model), F32), ((pheno, other), F32), tile]
    outs = call(back0, outs, got, genotypes, centre, phenotypes, keep, cols)
    send, start, mean, weight, back, scores, own = outs
    got = exchange(send, "var")
    outs = [((along * CORES,) + half, BF16), ((pheno, rows), F32)]
    send, image = call(project_kernel, outs, got, genotypes, mean)
    (send,) = call(middle_kernel, [((NEAR,) + half, BF16)], exchange(send, "samp", planes))
    got = exchange(send, "samp", lines)
    kept = (got, genotypes, mean, weight, back, own, cols, scores)
    out, sem = ((pheno, other), F32), (pltpu.SemaphoreType.DMA,)
    send, scores = call(back1_kernel, [((ways, pheno, LANE), F32)], *kept, out=out, scratch=sem)
    got = exchange(send, "var")
    part = ((pheno, rows // ways), F32)
    out, residual = call(finish_kernel, [part, part], got, start, image, norm, cols, make=jax.ShapeDtypeStruct)
    return (out, residual, scores)


def solution(mesh):
    in_specs = (
        P("samp", "var"),
        P("samp", "var"),
        P("samp"),
        P(None, "samp"),
        P(None, "samp"),
        P(),
        P(),
    )
    out_specs = (P(None, ("samp", "var")), P(None, ("samp", "var")), P(None, "var"))
    return jax.shard_map(shards, mesh=mesh, in_specs=in_specs, out_specs=out_specs, check_vma=False)
```

```python
import functools

import jax
import jax.numpy as jnp
from jax import lax
from jax.experimental import pallas as pl
from jax.experimental.pallas import tpu as pltpu
from jax.sharding import PartitionSpec as P

M = 40960
CENTRES = 22
SLOTS = 12
LANE = 128
BASE = 4096.0
GRID = 64.0
STEPS = 2
GRANT = 16 << 20
NEAR, CORES = 4, 2
BF16, F32 = jnp.bfloat16, jnp.float32
NT = (((1,), (1,)), ((), ()))


def split(x, parts):
    out = []
    for _ in range(parts):
        top = x.astype(BF16)
        out.append(top)
        x = x - top.astype(F32)
    return out


def dot(x, y):
    return jnp.dot(x, y, preferred_element_type=F32)


def dot_t(x, y):
    return lax.dot_general(x, y, NT, preferred_element_type=F32)


def iota(shape, dim):
    return lax.broadcasted_iota(jnp.int32, shape, dim)


def row_sum(x):
    return jnp.sum(x, axis=1, keepdims=True)


def in_lanes(columns):
    lane = iota((columns[0].shape[0], LANE), 1)
    out = jnp.zeros((columns[0].shape[0], LANE), F32)
    for at, column in enumerate(columns):
        out = jnp.where(lane == at, column, out)
    return out


def cut(x, at):
    return x[:, at * LANE : (at + 1) * LANE]


def square_sum(ref, top, deep, first, wide):
    acc = None
    for at in range(top, top + deep, 16):
        part = ref[at : at + 16, first : first + wide]
        acc = part * part if acc is None else acc + part * part
    return jnp.sum(acc.astype(F32), axis=0, keepdims=True)


def gather_kernel(
    gen_hbm, imp_hbm, centre_hbm, phen_hbm, earl_hbm, genetic_hbm, noise_hbm,
    out_ref, gen_ref, cols_ref, imp_ref, centre_ref, phen_ref, earl_ref, scal_ref, left_ref, right_ref, model_ref, other_ref, sem,
):
    rows, model = gen_ref.shape
    groups, pheno = out_ref.shape[0], phen_ref.shape[0]
    extra = imp_ref.shape[1]
    deep, wide = rows // STEPS, 2 * LANE
    span, side = model // groups, extra // groups
    small = [(centre_hbm, centre_ref), (phen_hbm, phen_ref), (earl_hbm, earl_ref)]
    small += [(genetic_hbm, scal_ref.at[0]), (noise_hbm, scal_ref.at[1])]
    copies = [pltpu.make_async_copy(x, y, sem.at[i]) for i, (x, y) in enumerate(small)]
    for step in range(STEPS):
        part = pl.ds(step * deep, deep)
        copies.append(pltpu.make_async_copy(gen_hbm.at[part], gen_ref.at[part], sem.at[5 + 2 * step]))
        copies.append(pltpu.make_async_copy(imp_hbm.at[part], imp_ref.at[part], sem.at[6 + 2 * step]))
    for copy in copies:
        copy.start()

    spot = iota((LANE, rows), 0)
    slot = iota((16, rows), 0)
    for copy in copies[:3]:
        copy.wait()
    centre = centre_ref[...]
    pairs = jnp.where(slot < SLOTS, jnp.where(centre == slot, 1.0, jnp.where(centre == slot + SLOTS, BASE, 0.0)), 0.0)
    pieces = [p.astype(F32) for p in split(phen_ref[...], 3)]
    phen = jnp.concatenate(pieces + [jnp.ones((pheno, rows), F32)], axis=0).astype(BF16)
    left_ref[...] = jnp.concatenate(pieces + [pairs], axis=0).astype(BF16)
    earl = earl_ref[...]
    pieces = [p.astype(F32) for p in split(earl, 3)]
    right_ref[...] = jnp.concatenate(pieces + [jnp.ones((pheno, rows), F32)], axis=0).astype(BF16)
    sums = []
    here = jnp.where(spot == centre, 1.0, 0.0).astype(BF16)
    full = dot_t(phen, here)
    row, lane = iota((pheno, LANE), 0), iota((pheno, LANE), 1)
    sums, count = full[0:8] + full[8:16] + full[16:24], full[24:32]
    own_mean = sums / jnp.maximum(count, 1.0)
    full = dot(jnp.concatenate([p.astype(F32) for p in split(own_mean, 3)], axis=0).astype(BF16), here)
    apart = phen_ref[...] - (full[0:8] + full[8:16] + full[16:24])
    within = row_sum(apart * apart)
    table = pltpu.roll(sums, span, 1) + pltpu.roll(count, span + CENTRES, 1)
    table = table + pltpu.roll(in_lanes([within, row_sum(earl), row_sum(earl * earl)]), span + 2 * CENTRES, 1)
    for copy in copies[3:5]:
        copy.wait()
    for at in range(2):
        column = jnp.zeros((pheno, LANE), F32)
        for k in range(pheno):
            column = jnp.where(row == k, scal_ref[at, k], column)
        cols_ref[at] = column * (1.0 / M) if at == 0 else column

    for step in range(STEPS):
        top, last = step * deep, step == STEPS - 1
        copies[5 + 2 * step].wait()
        for first in range(0, model, wide):
            cols = slice(first, first + wide)
            full = dot(left_ref[:, top : top + deep], gen_ref[top : top + deep, cols])
            square = square_sum(gen_ref, top, deep, first, wide) * BASE
            tail = full[32:40] + jnp.where(iota((pheno, wide), 0) == CENTRES - SLOTS - 8, square, 0.0)
            for place, part in ((0, full[0:8] + full[8:16] + full[16:24]), (8, full[24:32]), (16, tail)):
                model_ref[place : place + 8, cols] = part + model_ref[place : place + 8, cols] if step else part
        copies[6 + 2 * step].wait()
        for first in range(0, extra, wide):
            cols = slice(first, first + wide)
            full = dot(right_ref[:, top : top + deep], imp_ref[top : top + deep, cols])
            square = square_sum(imp_ref, top, deep, first, wide)
            lines = iota((pheno, wide), 0)
            counts = jnp.where(lines == 0, full[24:32], jnp.where(lines == 1, square, 0.0))
            for place, part in ((0, full[0:8] + full[8:16] + full[16:24]), (8, counts)):
                other_ref[place : place + 8, cols] = part + other_ref[place : place + 8, cols] if step else part

    def window(ref, place, first, width, to):
        block, skip = divmod(first, LANE)
        turn = (to - skip) % LANE
        out = pltpu.roll(ref[place : place + 8, block * LANE : (block + 1) * LANE], turn, 1)
        if skip + width > LANE:
            more = pltpu.roll(ref[place : place + 8, (block + 1) * LANE : (block + 2) * LANE], turn, 1)
            out = jnp.where(lane < to + LANE - skip, out, more)
        return out

    for at in range(groups):
        mine = lambda place: window(model_ref, place, at * span, span, 0)
        more = lambda place: jnp.where(lane < span + side, window(other_ref, place, at * side, side, span), 0.0)
        top = jnp.where(lane < span, mine(0), more(0))
        centre_rows = jnp.where(lane < span, mine(8), table)
        tail = jnp.where(lane < span, mine(16), more(8))
        for place, part in enumerate((top[0:4], top[4:8], centre_rows[0:4], centre_rows[4:8], tail[0:4])):
            out_ref[at, :, place * LANE : (place + 1) * LANE] = part


def gather(groups, *operands):
    genotypes, imputed, _, phenotypes = operands[:4]
    rows, model = genotypes.shape
    other = imputed.shape[1]
    pheno = phenotypes.shape[0]
    return pl.pallas_call(
        gather_kernel,
        out_shape=[
            pltpu.VMEM((groups, 4, 5 * LANE), F32),
            pltpu.VMEM((rows, model), BF16),
            pltpu.VMEM((2, pheno, LANE), F32),
        ],
        in_specs=[pl.BlockSpec(memory_space=pltpu.HBM)] * len(operands),
        out_specs=[pl.BlockSpec(memory_space=pltpu.VMEM)] * 3,
        scratch_shapes=[
            pltpu.VMEM((rows, other), BF16),
            pltpu.VMEM((1, rows), jnp.int32),
            pltpu.VMEM((pheno, rows), F32),
            pltpu.VMEM((pheno, rows), F32),
            pltpu.SMEM((2, pheno), F32),
            pltpu.VMEM((40, rows), BF16),
            pltpu.VMEM((32, rows), BF16),
            pltpu.VMEM((24, model), F32),
            pltpu.VMEM((16, other), F32),
            pltpu.SemaphoreType.DMA((5 + 2 * STEPS,)),
        ],
        compiler_params=pltpu.CompilerParams(vmem_limit_bytes=GRANT),
    )(*[pltpu.with_memory_space_constraint(x, pltpu.HBM) for x in operands])


def call(kernel, outs, *operands, make=pltpu.VMEM, out=None, scratch=()):
    out_shape = [make(shape, kind) for shape, kind in outs]
    out_specs = [pl.BlockSpec(memory_space=pltpu.VMEM)] * len(outs)
    if out is not None:
        out_shape.append(jax.ShapeDtypeStruct(*out))
        out_specs.append(pl.BlockSpec(memory_space=pltpu.HBM))
    return pl.pallas_call(
        kernel,
        out_shape=out_shape,
        in_specs=[pl.BlockSpec(memory_space=pltpu.VMEM)] * len(operands),
        out_specs=out_specs,
        scratch_shapes=scratch,
        compiler_params=pltpu.CompilerParams(vmem_limit_bytes=GRANT),
    )(*[pltpu.with_memory_space_constraint(x, pltpu.VMEM) for x in operands])


def owner_kernel(total, span, side, got_ref, cols_ref, send_ref, keep_ref, norm_ref):
    groups, pheno = got_ref.shape[0], 8
    row, lane = iota((pheno, LANE), 0), iota((pheno, LANE), 1)
    pieces = [got_ref[:, :, at * LANE : (at + 1) * LANE] for at in range(5)]
    raw = [jnp.sum(x, axis=0) for x in pieces]
    coarse = [jnp.floor(x * GRID) * (1.0 / GRID) for x in pieces[0:2]]
    rest = jnp.concatenate([jnp.sum(x - y, axis=0) for x, y in zip(pieces[0:2], coarse)], axis=0)
    coarse = jnp.concatenate([jnp.sum(y, axis=0) for y in coarse], axis=0)
    tops = [jnp.floor(x * (1.0 / BASE)) for x in pieces[2:]]
    low = jnp.concatenate([jnp.sum(x - BASE * y, axis=0) for x, y in zip(pieces[2:], tops)], axis=0)
    high = jnp.concatenate([jnp.sum(y, axis=0) for y in tops], axis=0)
    product = coarse + rest
    table = jnp.concatenate(raw[2:4], axis=0)
    sums = jnp.where(lane < CENTRES, pltpu.roll(table, LANE - span, 1), 0.0)
    count = jnp.where(lane < CENTRES, pltpu.roll(table, LANE - span - CENTRES, 1), 0.0)
    centre_mean = sums / jnp.maximum(count, 1.0)
    left = row_sum(sums - centre_mean * count)
    extra = span + 2 * CENTRES
    within, first, second = [table[:, extra + at : extra + at + 1] for at in range(3)]

    mean_top = jnp.floor(centre_mean * GRID + 0.5) * (1.0 / GRID)
    mean_rest = centre_mean - mean_top
    seen = jnp.zeros((1, LANE), F32)
    for c in range(CENTRES):
        line = low[c : c + 1] if c < SLOTS else high[c - SLOTS : c - SLOTS + 1]
        seen = seen + line
        coarse = coarse - mean_top[:, c : c + 1] * line
        rest = rest - mean_rest[:, c : c + 1] * line
    mean = seen / total
    variance = high[CENTRES - SLOTS : CENTRES - SLOTS + 1] / total - mean * mean
    spread = variance + 1e-05
    scale = jnp.where(variance == 0.0, 0.0, lax.rsqrt(spread))
    back = ((coarse + rest) - left * mean) * (scale * scale) * cols_ref[0]
    lines = jnp.zeros((pheno, LANE), F32)
    for at, line in enumerate(split(mean, 3) + split(scale * scale, 3) + split(spread, 2)):
        lines = jnp.where(row == at, line.astype(F32), lines)

    other_mean = raw[4][0:1] / total
    other_var = raw[4][1:2] / total - other_mean * other_mean + 1e-05
    earlier_var = second / total + 1e-05
    score = (product - first * other_mean) / jnp.sqrt(total * other_var * earlier_var)
    score_top = score.astype(BF16).astype(F32)

    here, there = lane < span, lane < span + side
    top = jnp.where(here, back, jnp.where(there, score_top, 0.0))
    under = jnp.where(here, lines, jnp.where(there, score - score_top, 0.0))
    send = jnp.concatenate([top, under], axis=0).astype(BF16)
    send_ref[...] = jnp.broadcast_to(send[None], (groups, 16, LANE))
    keep_ref[...] = centre_mean

    middle = pltpu.roll(centre_mean, span, 1)
    halves = []
    for half in range(2):
        between = jnp.zeros((pheno // 2, LANE), F32)
        for at in range(groups):
            part = got_ref[at, :, (2 + half) * LANE : (3 + half) * LANE]
            counted = pltpu.roll(part, LANE - CENTRES, 1)
            apart = part - counted * middle[4 * half : 4 * half + 4]
            between = between + apart * apart / jnp.maximum(counted, 1.0)
        halves.append(between)
    between = jnp.concatenate(halves, axis=0)
    between = jnp.where((lane >= span) & (lane < span + CENTRES), between, 0.0)
    norm_ref[...] = jnp.broadcast_to(row_sum(between) + within, (pheno, LANE))


def back0_kernel(
    span, side, got_ref, gen_ref, centre_ref, phen_ref, keep_ref, cols_ref,
    send_ref, start_ref, mean_ref, weight_ref, back_ref, score_ref, own_ref,
):
    ways = send_ref.shape[0]
    pheno, rows = phen_ref.shape
    model, other = gen_ref.shape[1], score_ref.shape[1]

    def block_of(at, width, skip, rows, load):
        lane = iota((rows, LANE), 1)
        out = None
        for owner in range(at * LANE // width, ((at + 1) * LANE - 1) // width + 1):
            first = owner * width - at * LANE
            part = pltpu.roll(load(owner), (first - skip) % LANE, 1)
            out = part if out is None else jnp.where(lane < first, out, part)
        return out

    shift = jnp.zeros((pheno, LANE), F32)
    own = jnp.zeros((pheno, LANE), F32)
    acc = None
    for pair in range(0, model // LANE, 2):
        values = []
        for at in (pair, pair + 1):
            block = block_of(at, span, 0, 16, lambda owner: got_ref[owner].astype(F32))
            cols = slice(at * LANE, (at + 1) * LANE)
            mean = block[8:9] + block[9:10] + block[10:11]
            mean_ref[:, cols] = mean
            weight_ref[:, cols] = block[11:12] + block[12:13] + block[13:14]
            back_ref[:, cols] = block[0:8]
            shift = shift + block[0:8] * mean
            own = own + block[0:8] * block[0:8] * (block[14:15] + block[15:16])
            values.append(block.astype(BF16))
        part = dot_t(jnp.concatenate(values, axis=1), gen_ref[:, pair * LANE : (pair + 2) * LANE])
        acc = part if acc is None else acc + part
    part = acc[0:8] - row_sum(shift)
    own_ref[...] = in_lanes([row_sum(own) / cols_ref[0][:, 0:1]])
    half = rows // 2
    send = jnp.concatenate([part[:, :half], part[:, half:]], axis=0).astype(BF16)
    send_ref[...] = jnp.broadcast_to(send[None], (ways, 16, half))
    for at in range(other // LANE):
        load = lambda owner: got_ref[owner].astype(F32)[0:8] + got_ref[owner].astype(F32)[8:16]
        score_ref[:, at * LANE : (at + 1) * LANE] = block_of(at, side, span, pheno, load)
    centre = centre_ref[...]
    start = phen_ref[...]
    centre_mean = keep_ref[...]
    for c in range(CENTRES):
        start = start - jnp.where(centre == c, centre_mean[:, c : c + 1], 0.0)
    start_ref[...] = start


def project_kernel(got_ref, gen_ref, mean_ref, send_ref, image_ref):
    peers = send_ref.shape[0]
    both = jnp.sum(got_ref[...].astype(F32), axis=0)
    image = jnp.concatenate([both[0:8], both[8:16]], axis=1)
    image_ref[...] = image
    pieces = [p.astype(F32) for p in split(image, 2)]
    total = row_sum(pieces[0] + pieces[1])
    left = jnp.concatenate(pieces, axis=0).astype(BF16)
    half = gen_ref.shape[1] // 2
    for at in range(0, half, 2 * LANE):
        parts = []
        for first in (at, at + half):
            cols = slice(first, first + 2 * LANE)
            full = dot(left, gen_ref[:, cols])
            parts.append(full[0:8] + full[8:16] - total * mean_ref[:, cols])
        send = jnp.concatenate(parts, axis=0).astype(BF16)
        for peer in range(peers):
            send_ref[peer, :, at : at + 2 * LANE] = send


def middle_kernel(got_ref, send_ref):
    got = jnp.sum(got_ref[...].astype(F32), axis=0)
    send_ref[...] = jnp.broadcast_to(got.astype(BF16)[None], send_ref.shape)


def back1_kernel(
    got_ref, gen_ref, mean_ref, weight_ref, back_ref, own_ref, cols_ref, score_ref, send_ref, out_hbm, sem
):
    copy = pltpu.make_async_copy(score_ref, out_hbm, sem)
    copy.start()
    ways, pheno, _ = send_ref.shape
    rows, model = gen_ref.shape
    half = model // 2
    wide = 2 * LANE
    genetic = cols_ref[0][:, 0:1]
    shift = jnp.zeros((pheno, wide), F32)
    new = jnp.zeros((pheno, wide), F32)
    mixed = jnp.zeros((pheno, wide), F32)
    acc = None
    for at in range(0, half, wide):
        got = jnp.sum(got_ref[:, :, at : at + wide].astype(F32), axis=0)
        for proj, first in ((got[0:8], at), (got[8:16], at + half)):
            cols = slice(first, first + wide)
            back = proj * weight_ref[:, cols] * genetic
            new = new + proj * back
            mixed = mixed + proj * back_ref[:, cols]
            pieces = [p.astype(F32) for p in split(back, 2)]
            shift = shift + (pieces[0] + pieces[1]) * mean_ref[:, cols]
            low = jnp.concatenate(pieces, axis=0).astype(BF16)
            part = dot_t(low, gen_ref[:, cols])
            acc = part if acc is None else acc + part
    part = acc[0:8] + acc[8:16] - row_sum(shift)
    energies = (own_ref[...][:, 0:1], row_sum(mixed), row_sum(new))
    width = rows // ways
    per = LANE // width
    lane = iota((pheno, LANE), 1)
    for peer in range(ways):
        send = cut(part, peer // per)
        for at, energy in enumerate(energies):
            send = jnp.where(lane == (width * (peer % per) + width + at) % LANE, energy, send)
        send_ref[peer] = send
    copy.wait()


def finish_kernel(got_ref, start_ref, image_ref, norm_ref, cols_ref, out_ref, residual_ref):
    ways, pheno, _ = got_ref.shape
    rows = start_ref.shape[1]
    width = rows // ways
    per = LANE // width
    mine = lax.axis_index("var")
    tile, at = lax.div(mine, per), lax.rem(mine, per)
    got = jnp.sum(got_ref[...], axis=0)
    lane = iota((pheno, LANE), 1)
    spots = [lax.rem(at * width + width + i, LANE) for i in range(3)]
    cross, square, cube = [row_sum(jnp.where(lane == spot, got, 0.0)) for spot in spots]
    norm0, noise = norm_ref[...][:, 0:1], cols_ref[1][:, 0:1]
    rate = cross / norm0
    alpha0 = 1.0 / (rate + noise)
    norm1 = alpha0 * alpha0 * (square - rate * cross)
    on_image, on_start = -alpha0, alpha0 * rate + norm1 / norm0
    both, first, last = on_image * on_image, 2.0 * on_image * on_start, on_start * on_start
    length = both * square + first * cross + last * norm0
    curve = both * cube + first * square + last * cross
    alpha1 = norm1 / (curve + noise * length)
    start = jnp.zeros((pheno, LANE), F32)
    image = jnp.zeros((pheno, LANE), F32)
    for t in range(rows // LANE):
        start = jnp.where(tile == t, cut(start_ref[...], t), start)
        image = jnp.where(tile == t, cut(image_ref[...], t), image)
    direction = on_image * image + on_start * start
    residual = -alpha0 * (image - rate * start) - alpha1 * (on_image * got + on_start * image + noise * direction)
    answer = alpha0 * start + alpha1 * direction
    out, left = answer[:, :width], residual[:, :width]
    for a in range(1, per):
        out = jnp.where(at == a, answer[:, a * width : (a + 1) * width], out)
        left = jnp.where(at == a, residual[:, a * width : (a + 1) * width], left)
    out_ref[...] = out
    residual_ref[...] = left


def exchange(x, axis, sets=None):
    return lax.all_to_all(x, axis, 0, 0, axis_index_groups=sets, tiled=True)


def shards(genotypes, imputed, centre, phenotypes, earlier, genetic, noise):
    rows, model = genotypes.shape
    other = imputed.shape[1]
    pheno = phenotypes.shape[0]
    groups, ways = lax.axis_size("samp"), lax.axis_size("var")
    span, side = model // groups, other // groups
    centre = centre[None, :]
    along = groups // (NEAR * CORES)
    at = lambda x, y, core: (x * NEAR + y) * CORES + core
    planes = [[at(x, y, core) for x in range(along) for core in range(CORES)] for y in range(NEAR)]
    lines = [[at(x, y, core) for y in range(NEAR)] for x in range(along) for core in range(CORES)]
    half = (16, model // 2)

    send, genotypes, cols = gather(groups, genotypes, imputed, centre, phenotypes, earlier, genetic, noise)
    got = exchange(send, "samp")
    owner = functools.partial(owner_kernel, float(rows * groups), span, side)
    tile = ((pheno, LANE), F32)
    send, keep, norm = call(owner, [((groups, 16, LANE), BF16), tile, tile], got, cols)
    got = exchange(send, "samp")
    back0 = functools.partial(back0_kernel, span, side)
    row, wide = ((1, model), F32), ((pheno, rows), F32)
    outs = [((ways, 16, rows // 2), BF16), wide, row, row]
    outs += [((pheno, model), F32), ((pheno, other), F32), tile]
    outs = call(back0, outs, got, genotypes, centre, phenotypes, keep, cols)
    send, start, mean, weight, back, scores, own = outs
    got = exchange(send, "var")
    outs = [((along * CORES,) + half, BF16), ((pheno, rows), F32)]
    send, image = call(project_kernel, outs, got, genotypes, mean)
    (send,) = call(middle_kernel, [((NEAR,) + half, BF16)], exchange(send, "samp", planes))
    got = exchange(send, "samp", lines)
    kept = (got, genotypes, mean, weight, back, own, cols, scores)
    out, sem = ((pheno, other), F32), (pltpu.SemaphoreType.DMA,)
    send, scores = call(back1_kernel, [((ways, pheno, LANE), F32)], *kept, out=out, scratch=sem)
    got = exchange(send, "var")
    part = ((pheno, rows // ways), F32)
    out, residual = call(finish_kernel, [part, part], got, start, image, norm, cols, make=jax.ShapeDtypeStruct)
    return (out, residual, scores)


def solution(mesh):
    in_specs = (
        P("samp", "var"),
        P("samp", "var"),
        P("samp"),
        P(None, "samp"),
        P(None, "samp"),
        P(),
        P(),
    )
    out_specs = (P(None, ("samp", "var")), P(None, ("samp", "var")), P(None, "var"))
    return jax.shard_map(shards, mesh=mesh, in_specs=in_specs, out_specs=out_specs, check_vma=False)
```

```python
import functools

import jax
import jax.numpy as jnp
from jax import lax
from jax.experimental import pallas as pl
from jax.experimental.pallas import tpu as pltpu
from jax.sharding import PartitionSpec as P

M = 40960
CENTRES = 22
SLOTS = 12
LANE = 128
BASE = 4096.0
GRID = 64.0
STEPS = 2
GRANT = 16 << 20
NEAR, CORES = 4, 2
BF16, F32 = jnp.bfloat16, jnp.float32
NT = (((1,), (1,)), ((), ()))


def split(x, parts):
    out = []
    for _ in range(parts):
        top = x.astype(BF16)
        out.append(top)
        x = x - top.astype(F32)
    return out


def dot(x, y):
    return jnp.dot(x, y, preferred_element_type=F32)


def dot_t(x, y):
    return lax.dot_general(x, y, NT, preferred_element_type=F32)


def iota(shape, dim):
    return lax.broadcasted_iota(jnp.int32, shape, dim)


def row_sum(x):
    return jnp.sum(x, axis=1, keepdims=True)


def in_lanes(columns):
    lane = iota((columns[0].shape[0], LANE), 1)
    out = jnp.zeros((columns[0].shape[0], LANE), F32)
    for at, column in enumerate(columns):
        out = jnp.where(lane == at, column, out)
    return out


def cut(x, at):
    return x[:, at * LANE : (at + 1) * LANE]


def square_sum(ref, top, deep, first, wide):
    acc = None
    for at in range(top, top + deep, 16):
        part = ref[at : at + 16, first : first + wide]
        acc = part * part if acc is None else acc + part * part
    return jnp.sum(acc.astype(F32), axis=0, keepdims=True)


def gather_kernel(
    gen_hbm, imp_hbm, centre_hbm, phen_hbm, earl_hbm, genetic_hbm, noise_hbm,
    out_ref, gen_ref, cols_ref, imp_ref, centre_ref, phen_ref, earl_ref, scal_ref, left_ref, right_ref, model_ref, other_ref, sem,
):
    rows, model = gen_ref.shape
    groups, pheno = out_ref.shape[0], phen_ref.shape[0]
    extra = imp_ref.shape[1]
    deep, wide = rows // STEPS, 2 * LANE
    span, side = model // groups, extra // groups
    small = [(centre_hbm, centre_ref), (phen_hbm, phen_ref), (earl_hbm, earl_ref)]
    small += [(genetic_hbm, scal_ref.at[0]), (noise_hbm, scal_ref.at[1])]
    copies = [pltpu.make_async_copy(x, y, sem.at[i]) for i, (x, y) in enumerate(small)]
    for step in range(STEPS):
        part = pl.ds(step * deep, deep)
        copies.append(pltpu.make_async_copy(gen_hbm.at[part], gen_ref.at[part], sem.at[5 + 2 * step]))
        copies.append(pltpu.make_async_copy(imp_hbm.at[part], imp_ref.at[part], sem.at[6 + 2 * step]))
    for copy in copies:
        copy.start()

    spot = iota((LANE, rows), 0)
    slot = iota((16, rows), 0)
    for copy in copies[:3]:
        copy.wait()
    centre = centre_ref[...]
    pairs = jnp.where(slot < SLOTS, jnp.where(centre == slot, 1.0, jnp.where(centre == slot + SLOTS, BASE, 0.0)), 0.0)
    pieces = [p.astype(F32) for p in split(phen_ref[...], 3)]
    phen = jnp.concatenate(pieces + [jnp.ones((pheno, rows), F32)], axis=0).astype(BF16)
    left_ref[...] = jnp.concatenate(pieces + [pairs], axis=0).astype(BF16)
    earl = earl_ref[...]
    pieces = [p.astype(F32) for p in split(earl, 3)]
    right_ref[...] = jnp.concatenate(pieces + [jnp.ones((pheno, rows), F32)], axis=0).astype(BF16)
    sums = []
    here = jnp.where(spot == centre, 1.0, 0.0).astype(BF16)
    full = dot_t(phen, here)
    row, lane = iota((pheno, LANE), 0), iota((pheno, LANE), 1)
    sums, count = full[0:8] + full[8:16] + full[16:24], full[24:32]
    own_mean = sums / jnp.maximum(count, 1.0)
    full = dot(jnp.concatenate([p.astype(F32) for p in split(own_mean, 3)], axis=0).astype(BF16), here)
    apart = phen_ref[...] - (full[0:8] + full[8:16] + full[16:24])
    within = row_sum(apart * apart)
    table = pltpu.roll(sums, span, 1) + pltpu.roll(count, span + CENTRES, 1)
    table = table + pltpu.roll(in_lanes([within, row_sum(earl), row_sum(earl * earl)]), span + 2 * CENTRES, 1)
    for copy in copies[3:5]:
        copy.wait()
    for at in range(2):
        column = jnp.zeros((pheno, LANE), F32)
        for k in range(pheno):
            column = jnp.where(row == k, scal_ref[at, k], column)
        cols_ref[at] = column * (1.0 / M) if at == 0 else column

    for step in range(STEPS):
        top, last = step * deep, step == STEPS - 1
        copies[5 + 2 * step].wait()
        for first in range(0, model, wide):
            cols = slice(first, first + wide)
            full = dot(left_ref[:, top : top + deep], gen_ref[top : top + deep, cols])
            square = square_sum(gen_ref, top, deep, first, wide) * BASE
            tail = full[32:40] + jnp.where(iota((pheno, wide), 0) == CENTRES - SLOTS - 8, square, 0.0)
            for place, part in ((0, full[0:8] + full[8:16] + full[16:24]), (8, full[24:32]), (16, tail)):
                model_ref[place : place + 8, cols] = part + model_ref[place : place + 8, cols] if step else part
        copies[6 + 2 * step].wait()
        for first in range(0, extra, wide):
            cols = slice(first, first + wide)
            full = dot(right_ref[:, top : top + deep], imp_ref[top : top + deep, cols])
            square = square_sum(imp_ref, top, deep, first, wide)
            lines = iota((pheno, wide), 0)
            counts = jnp.where(lines == 0, full[24:32], jnp.where(lines == 1, square, 0.0))
            for place, part in ((0, full[0:8] + full[8:16] + full[16:24]), (8, counts)):
                other_ref[place : place + 8, cols] = part + other_ref[place : place + 8, cols] if step else part

    def window(ref, place, first, width, to):
        block, skip = divmod(first, LANE)
        turn = (to - skip) % LANE
        out = pltpu.roll(ref[place : place + 8, block * LANE : (block + 1) * LANE], turn, 1)
        if skip + width > LANE:
            more = pltpu.roll(ref[place : place + 8, (block + 1) * LANE : (block + 2) * LANE], turn, 1)
            out = jnp.where(lane < to + LANE - skip, out, more)
        return out

    for at in range(groups):
        mine = lambda place: window(model_ref, place, at * span, span, 0)
        more = lambda place: jnp.where(lane < span + side, window(other_ref, place, at * side, side, span), 0.0)
        top = jnp.where(lane < span, mine(0), more(0))
        centre_rows = jnp.where(lane < span, mine(8), table)
        tail = jnp.where(lane < span, mine(16), more(8))
        for place, part in enumerate((top[0:4], top[4:8], centre_rows[0:4], centre_rows[4:8], tail[0:4])):
            out_ref[at, :, place * LANE : (place + 1) * LANE] = part


def gather(groups, *operands):
    genotypes, imputed, _, phenotypes = operands[:4]
    rows, model = genotypes.shape
    other = imputed.shape[1]
    pheno = phenotypes.shape[0]
    return pl.pallas_call(
        gather_kernel,
        out_shape=[
            pltpu.VMEM((groups, 4, 5 * LANE), F32),
            pltpu.VMEM((rows, model), BF16),
            pltpu.VMEM((2, pheno, LANE), F32),
        ],
        in_specs=[pl.BlockSpec(memory_space=pltpu.HBM)] * len(operands),
        out_specs=[pl.BlockSpec(memory_space=pltpu.VMEM)] * 3,
        scratch_shapes=[
            pltpu.VMEM((rows, other), BF16),
            pltpu.VMEM((1, rows), jnp.int32),
            pltpu.VMEM((pheno, rows), F32),
            pltpu.VMEM((pheno, rows), F32),
            pltpu.SMEM((2, pheno), F32),
            pltpu.VMEM((40, rows), BF16),
            pltpu.VMEM((32, rows), BF16),
            pltpu.VMEM((24, model), F32),
            pltpu.VMEM((16, other), F32),
            pltpu.SemaphoreType.DMA((5 + 2 * STEPS,)),
        ],
        compiler_params=pltpu.CompilerParams(vmem_limit_bytes=GRANT),
    )(*[pltpu.with_memory_space_constraint(x, pltpu.HBM) for x in operands])


def call(kernel, outs, *operands, make=pltpu.VMEM, out=None, scratch=()):
    out_shape = [make(shape, kind) for shape, kind in outs]
    out_specs = [pl.BlockSpec(memory_space=pltpu.VMEM)] * len(outs)
    if out is not None:
        out_shape.append(jax.ShapeDtypeStruct(*out))
        out_specs.append(pl.BlockSpec(memory_space=pltpu.HBM))
    return pl.pallas_call(
        kernel,
        out_shape=out_shape,
        in_specs=[pl.BlockSpec(memory_space=pltpu.VMEM)] * len(operands),
        out_specs=out_specs,
        scratch_shapes=scratch,
        compiler_params=pltpu.CompilerParams(vmem_limit_bytes=GRANT),
    )(*[pltpu.with_memory_space_constraint(x, pltpu.VMEM) for x in operands])


def owner_kernel(total, span, side, got_ref, cols_ref, send_ref, keep_ref, norm_ref):
    groups, pheno = got_ref.shape[0], 8
    row, lane = iota((pheno, LANE), 0), iota((pheno, LANE), 1)
    pieces = [got_ref[:, :, at * LANE : (at + 1) * LANE] for at in range(5)]
    raw = [jnp.sum(x, axis=0) for x in pieces]
    coarse = [jnp.floor(x * GRID) * (1.0 / GRID) for x in pieces[0:2]]
    rest = jnp.concatenate([jnp.sum(x - y, axis=0) for x, y in zip(pieces[0:2], coarse)], axis=0)
    coarse = jnp.concatenate([jnp.sum(y, axis=0) for y in coarse], axis=0)
    tops = [jnp.floor(x * (1.0 / BASE)) for x in pieces[2:]]
    low = jnp.concatenate([jnp.sum(x - BASE * y, axis=0) for x, y in zip(pieces[2:], tops)], axis=0)
    high = jnp.concatenate([jnp.sum(y, axis=0) for y in tops], axis=0)
    product = coarse + rest
    table = jnp.concatenate(raw[2:4], axis=0)
    sums = jnp.where(lane < CENTRES, pltpu.roll(table, LANE - span, 1), 0.0)
    count = jnp.where(lane < CENTRES, pltpu.roll(table, LANE - span - CENTRES, 1), 0.0)
    centre_mean = sums / jnp.maximum(count, 1.0)
    left = row_sum(sums - centre_mean * count)
    extra = span + 2 * CENTRES
    within, first, second = [table[:, extra + at : extra + at + 1] for at in range(3)]

    mean_top = jnp.floor(centre_mean * GRID + 0.5) * (1.0 / GRID)
    mean_rest = centre_mean - mean_top
    seen = jnp.zeros((1, LANE), F32)
    for c in range(CENTRES):
        line = low[c : c + 1] if c < SLOTS else high[c - SLOTS : c - SLOTS + 1]
        seen = seen + line
        coarse = coarse - mean_top[:, c : c + 1] * line
        rest = rest - mean_rest[:, c : c + 1] * line
    mean = seen / total
    variance = high[CENTRES - SLOTS : CENTRES - SLOTS + 1] / total - mean * mean
    spread = variance + 1e-05
    scale = jnp.where(variance == 0.0, 0.0, lax.rsqrt(spread))
    back = ((coarse + rest) - left * mean) * (scale * scale) * cols_ref[0]
    lines = jnp.zeros((pheno, LANE), F32)
    for at, line in enumerate(split(mean, 3) + split(scale * scale, 3) + split(spread, 2)):
        lines = jnp.where(row == at, line.astype(F32), lines)

    other_mean = raw[4][0:1] / total
    other_var = raw[4][1:2] / total - other_mean * other_mean + 1e-05
    earlier_var = second / total + 1e-05
    score = (product - first * other_mean) / jnp.sqrt(total * other_var * earlier_var)
    score_top = score.astype(BF16).astype(F32)

    here, there = lane < span, lane < span + side
    top = jnp.where(here, back, jnp.where(there, score_top, 0.0))
    under = jnp.where(here, lines, jnp.where(there, score - score_top, 0.0))
    send = jnp.concatenate([top, under], axis=0).astype(BF16)
    send_ref[...] = jnp.broadcast_to(send[None], (groups, 16, LANE))
    keep_ref[...] = centre_mean

    middle = pltpu.roll(centre_mean, span, 1)
    halves = []
    for half in range(2):
        between = jnp.zeros((pheno // 2, LANE), F32)
        for at in range(groups):
            part = got_ref[at, :, (2 + half) * LANE : (3 + half) * LANE]
            counted = pltpu.roll(part, LANE - CENTRES, 1)
            apart = part - counted * middle[4 * half : 4 * half + 4]
            between = between + apart * apart / jnp.maximum(counted, 1.0)
        halves.append(between)
    between = jnp.concatenate(halves, axis=0)
    between = jnp.where((lane >= span) & (lane < span + CENTRES), between, 0.0)
    norm_ref[...] = jnp.broadcast_to(row_sum(between) + within, (pheno, LANE))


def back0_kernel(
    span, side, got_ref, gen_ref, centre_ref, phen_ref, keep_ref, cols_ref,
    send_ref, start_ref, mean_ref, weight_ref, back_ref, score_ref, own_ref,
):
    ways = send_ref.shape[0]
    pheno, rows = phen_ref.shape
    model, other = gen_ref.shape[1], score_ref.shape[1]

    def block_of(at, width, skip, rows, load):
        lane = iota((rows, LANE), 1)
        out = None
        for owner in range(at * LANE // width, ((at + 1) * LANE - 1) // width + 1):
            first = owner * width - at * LANE
            part = pltpu.roll(load(owner), (first - skip) % LANE, 1)
            out = part if out is None else jnp.where(lane < first, out, part)
        return out

    shift = jnp.zeros((pheno, LANE), F32)
    own = jnp.zeros((pheno, LANE), F32)
    acc = None
    for pair in range(0, model // LANE, 2):
        values = []
        for at in (pair, pair + 1):
            block = block_of(at, span, 0, 16, lambda owner: got_ref[owner].astype(F32))
            cols = slice(at * LANE, (at + 1) * LANE)
            mean = block[8:9] + block[9:10] + block[10:11]
            mean_ref[:, cols] = mean
            weight_ref[:, cols] = block[11:12] + block[12:13] + block[13:14]
            back_ref[:, cols] = block[0:8]
            shift = shift + block[0:8] * mean
            own = own + block[0:8] * block[0:8] * (block[14:15] + block[15:16])
            values.append(block.astype(BF16))
        part = dot_t(jnp.concatenate(values, axis=1), gen_ref[:, pair * LANE : (pair + 2) * LANE])
        acc = part if acc is None else acc + part
    part = acc[0:8] - row_sum(shift)
    own_ref[...] = in_lanes([row_sum(own) / cols_ref[0][:, 0:1]])
    half = rows // 2
    send = jnp.concatenate([part[:, :half], part[:, half:]], axis=0).astype(BF16)
    send_ref[...] = jnp.broadcast_to(send[None], (ways, 16, half))
    for at in range(other // LANE):
        load = lambda owner: got_ref[owner].astype(F32)[0:8] + got_ref[owner].astype(F32)[8:16]
        score_ref[:, at * LANE : (at + 1) * LANE] = block_of(at, side, span, pheno, load)
    centre = centre_ref[...]
    start = phen_ref[...]
    centre_mean = keep_ref[...]
    for c in range(CENTRES):
        start = start - jnp.where(centre == c, centre_mean[:, c : c + 1], 0.0)
    start_ref[...] = start


def project_kernel(got_ref, gen_ref, mean_ref, send_ref, image_ref):
    peers = send_ref.shape[0]
    both = jnp.sum(got_ref[...].astype(F32), axis=0)
    image = jnp.concatenate([both[0:8], both[8:16]], axis=1)
    image_ref[...] = image
    pieces = [p.astype(F32) for p in split(image, 2)]
    total = row_sum(pieces[0] + pieces[1])
    left = jnp.concatenate(pieces, axis=0).astype(BF16)
    half = gen_ref.shape[1] // 2
    for at in range(0, half, 2 * LANE):
        parts = []
        for first in (at, at + half):
            cols = slice(first, first + 2 * LANE)
            full = dot(left, gen_ref[:, cols])
            parts.append(full[0:8] + full[8:16] - total * mean_ref[:, cols])
        send = jnp.concatenate(parts, axis=0).astype(BF16)
        for peer in range(peers):
            send_ref[peer, :, at : at + 2 * LANE] = send


def middle_kernel(got_ref, send_ref):
    got = jnp.sum(got_ref[...].astype(F32), axis=0)
    send_ref[...] = jnp.broadcast_to(got.astype(BF16)[None], send_ref.shape)


def back1_kernel(
    got_ref, gen_ref, mean_ref, weight_ref, back_ref, own_ref, cols_ref, score_ref, send_ref, out_hbm, sem
):
    copy = pltpu.make_async_copy(score_ref, out_hbm, sem)
    copy.start()
    ways, pheno, _ = send_ref.shape
    rows, model = gen_ref.shape
    half = model // 2
    wide = 2 * LANE
    genetic = cols_ref[0][:, 0:1]
    shift = jnp.zeros((pheno, wide), F32)
    new = jnp.zeros((pheno, wide), F32)
    mixed = jnp.zeros((pheno, wide), F32)
    acc = None
    for at in range(0, half, wide):
        got = jnp.sum(got_ref[:, :, at : at + wide].astype(F32), axis=0)
        for proj, first in ((got[0:8], at), (got[8:16], at + half)):
            cols = slice(first, first + wide)
            back = proj * weight_ref[:, cols] * genetic
            new = new + proj * back
            mixed = mixed + proj * back_ref[:, cols]
            pieces = [p.astype(F32) for p in split(back, 2)]
            shift = shift + (pieces[0] + pieces[1]) * mean_ref[:, cols]
            low = jnp.concatenate(pieces, axis=0).astype(BF16)
            part = dot_t(low, gen_ref[:, cols])
            acc = part if acc is None else acc + part
    part = acc[0:8] + acc[8:16] - row_sum(shift)
    energies = (own_ref[...][:, 0:1], row_sum(mixed), row_sum(new))
    width = rows // ways
    per = LANE // width
    lane = iota((pheno, LANE), 1)
    for peer in range(ways):
        send = cut(part, peer // per)
        for at, energy in enumerate(energies):
            send = jnp.where(lane == (width * (peer % per) + width + at) % LANE, energy, send)
        send_ref[peer] = send
    copy.wait()


def finish_kernel(got_ref, start_ref, image_ref, norm_ref, cols_ref, out_ref, residual_ref):
    ways, pheno, _ = got_ref.shape
    rows = start_ref.shape[1]
    width = rows // ways
    per = LANE // width
    mine = lax.axis_index("var")
    tile, at = lax.div(mine, per), lax.rem(mine, per)
    got = jnp.sum(got_ref[...], axis=0)
    lane = iota((pheno, LANE), 1)
    spots = [lax.rem(at * width + width + i, LANE) for i in range(3)]
    cross, square, cube = [row_sum(jnp.where(lane == spot, got, 0.0)) for spot in spots]
    norm0, noise = norm_ref[...][:, 0:1], cols_ref[1][:, 0:1]
    rate = cross / norm0
    alpha0 = 1.0 / (rate + noise)
    norm1 = alpha0 * alpha0 * (square - rate * cross)
    on_image, on_start = -alpha0, alpha0 * rate + norm1 / norm0
    both, first, last = on_image * on_image, 2.0 * on_image * on_start, on_start * on_start
    length = both * square + first * cross + last * norm0
    curve = both * cube + first * square + last * cross
    alpha1 = norm1 / (curve + noise * length)
    start = jnp.zeros((pheno, LANE), F32)
    image = jnp.zeros((pheno, LANE), F32)
    for t in range(rows // LANE):
        start = jnp.where(tile == t, cut(start_ref[...], t), start)
        image = jnp.where(tile == t, cut(image_ref[...], t), image)
    direction = on_image * image + on_start * start
    residual = -alpha0 * (image - rate * start) - alpha1 * (on_image * got + on_start * image + noise * direction)
    answer = alpha0 * start + alpha1 * direction
    turn = lax.rem(LANE - at * width, LANE)
    out_ref[...] = pltpu.roll(answer, turn, 1)[:, :width]
    residual_ref[...] = pltpu.roll(residual, turn, 1)[:, :width]


def exchange(x, axis, sets=None):
    return lax.all_to_all(x, axis, 0, 0, axis_index_groups=sets, tiled=True)


def shards(genotypes, imputed, centre, phenotypes, earlier, genetic, noise):
    rows, model = genotypes.shape
    other = imputed.shape[1]
    pheno = phenotypes.shape[0]
    groups, ways = lax.axis_size("samp"), lax.axis_size("var")
    span, side = model // groups, other // groups
    centre = centre[None, :]
    along = groups // (NEAR * CORES)
    at = lambda x, y, core: (x * NEAR + y) * CORES + core
    planes = [[at(x, y, core) for x in range(along) for core in range(CORES)] for y in range(NEAR)]
    lines = [[at(x, y, core) for y in range(NEAR)] for x in range(along) for core in range(CORES)]
    half = (16, model // 2)

    send, genotypes, cols = gather(groups, genotypes, imputed, centre, phenotypes, earlier, genetic, noise)
    got = exchange(send, "samp")
    owner = functools.partial(owner_kernel, float(rows * groups), span, side)
    tile = ((pheno, LANE), F32)
    send, keep, norm = call(owner, [((groups, 16, LANE), BF16), tile, tile], got, cols)
    got = exchange(send, "samp")
    back0 = functools.partial(back0_kernel, span, side)
    row, wide = ((1, model), F32), ((pheno, rows), F32)
    outs = [((ways, 16, rows // 2), BF16), wide, row, row]
    outs += [((pheno, model), F32), ((pheno, other), F32), tile]
    outs = call(back0, outs, got, genotypes, centre, phenotypes, keep, cols)
    send, start, mean, weight, back, scores, own = outs
    got = exchange(send, "var")
    outs = [((along * CORES,) + half, BF16), ((pheno, rows), F32)]
    send, image = call(project_kernel, outs, got, genotypes, mean)
    (send,) = call(middle_kernel, [((NEAR,) + half, BF16)], exchange(send, "samp", planes))
    got = exchange(send, "samp", lines)
    kept = (got, genotypes, mean, weight, back, own, cols, scores)
    out, sem = ((pheno, other), F32), (pltpu.SemaphoreType.DMA,)
    send, scores = call(back1_kernel, [((ways, pheno, LANE), F32)], *kept, out=out, scratch=sem)
    got = exchange(send, "var")
    part = ((pheno, rows // ways), F32)
    out, residual = call(finish_kernel, [part, part], got, start, image, norm, cols, make=jax.ShapeDtypeStruct)
    return (out, residual, scores)


def solution(mesh):
    in_specs = (
        P("samp", "var"),
        P("samp", "var"),
        P("samp"),
        P(None, "samp"),
        P(None, "samp"),
        P(),
        P(),
    )
    out_specs = (P(None, ("samp", "var")), P(None, ("samp", "var")), P(None, "var"))
    return jax.shard_map(shards, mesh=mesh, in_specs=in_specs, out_specs=out_specs, check_vma=False)
```
